32 devices in a mesh: role: 2 (over core), dev: 16 (over z, y, x).
Axes of the slice: x: 2, y: 2, z: 4, core: 2. Of those that a mesh axis runs over, the one named last changes fastest.
Arguments:
- positions: float32 [256, 3, 512], P(('role', 'dev')), may hold values from -1 to 1
- normals: float32 [256, 3, 512], P(('role', 'dev')), may hold values from -3.6 to 3.6
- panel_areas: float32 [256, 512], P(('role', 'dev')), may hold values from 0.005 to 0.05
- panel_counts: int32 [256], P(('role', 'dev')), may hold values from 128 to 512, as said below
- near_lists: int32 [256, 6], P(('role', 'dev')), may hold values from 0 to 255, as said below
- near_counts: int32 [256], P(('role', 'dev')), may hold values from 1 to 6
- leaf_lists: int32 [256, 16], P(('role', 'dev')), may hold values from 0 to 255, as said below
- leaf_kinds: int32 [256, 16], P(('role', 'dev')), may hold values from 0 to 7
- group_lists: int32 [32, 16], P(('role', 'dev')), may hold values from 0 to 31
- group_kinds: int32 [32, 16], P(('role', 'dev')), may hold values from 0 to 7
- block_inverse: bfloat16 [256, 512, 512], P(('role', 'dev')), may hold values from -1 to 3
- moment_maps: bfloat16 [256, 256, 512], P(('role', 'dev')), may hold values from -0.25 to 0.25
- up_operators: bfloat16 [8, 256, 256], replicated, may hold values from -0.125 to 0.125
- far_operators: bfloat16 [2, 8, 256, 256], replicated, may hold values from -0.09375 to 0.09375
- krylov_basis: float32 [8, 256, 512], P(None, ('role', 'dev')), may hold values from -64 to 64, as said below
Outputs:
- next_vector: float32 [256, 512], P(('role', 'dev'))
- hessenberg_column: float32 [9], replicated
The draws below stay inside these ranges and needn't reach their ends.
Inputs may be any that keep to these rules, and one draw needn't show every extreme that they name: `panel_counts`: some cluster has all 512 panels live. `near_lists`: ids of clusters held by the devices at most 3 places from the cluster's own device along role+dev; entries may repeat. `leaf_lists`: ids of clusters held by the devices at most 3 places from the cluster's own device along role+dev; entries may repeat. `krylov_basis`: the vectors are orthonormal under the mean over all 131072 entries, and zero on panels that are not live.
All inputs are finite; a program needn't handle non-finite values.
Results may differ from the reference program's by a relative error of at most 0.0044.
Values may be sent and summed in bfloat16 or wider, within the bound.
A program may use at most 64 MiB of HBM per device.

```python
import math
import jax
import jax.numpy as jnp
from jax import lax

P_SIZE = 512
C = 256
CL_DEV = 8
NNB = 6
NIL = 16
NOP = 8
KRY = 8
RADIUS = 3
CLUSTERS = 256
GROUPS = 32


def live_counts(key):
    counts = jax.random.randint(jax.random.fold_in(key, 101), (CLUSTERS,), P_SIZE // 4, P_SIZE + 1)
    chosen = jax.random.randint(jax.random.fold_in(key, 102), (), 0, CLUSTERS)
    return jnp.where(jnp.arange(CLUSTERS) == chosen, P_SIZE, counts).astype(jnp.int32)


def draw_panel_counts(key, part):
    return live_counts(key)


def window_lists(key, width):
    owners = jnp.arange(CLUSTERS, dtype=jnp.int32) // CL_DEV
    offsets = jax.random.randint(key, (CLUSTERS, width), 0, (2 * RADIUS + 1) * CL_DEV)
    listed = (owners[:, None] - RADIUS) * CL_DEV + offsets
    return jnp.clip(listed, 0, CLUSTERS - 1).astype(jnp.int32)


def draw_near_lists(key, part):
    return window_lists(jax.random.fold_in(key, 201), NNB)


def draw_leaf_lists(key, part):
    return window_lists(jax.random.fold_in(key, 202), NIL)


def draw_block_inverse(key, part):
    spread_key = jax.random.fold_in(key, 301)
    scale_key = jax.random.fold_in(key, 302)
    spread_part = jnp.clip(0.5 * jax.random.normal(spread_key, (CLUSTERS, P_SIZE, P_SIZE), jnp.float32), -3.0, 3.0)
    spread_part = spread_part * P_SIZE ** (-0.5)
    diagonal = jax.random.uniform(scale_key, (CLUSTERS, P_SIZE), jnp.float32, 1.0, 2.0)
    return (spread_part + diagonal[:, :, None] * jnp.eye(P_SIZE, dtype=jnp.float32)).astype(jnp.bfloat16)


def draw_krylov_basis(key, part):
    counts = live_counts(key)
    live = (jnp.arange(P_SIZE)[None, :] < counts[:, None]).astype(jnp.float32)
    drawn = jax.random.normal(jax.random.fold_in(key, 401), (KRY, CLUSTERS, P_SIZE), jnp.float32)
    drawn = drawn * live[None]
    entries = CLUSTERS * P_SIZE
    vectors = []
    for index_k in range(KRY):
        vector = drawn[index_k]
        for sweep in range(2):
            for earlier in vectors:
                vector = vector - jnp.sum(vector * earlier) / entries * earlier
        vector = vector * jnp.sqrt(entries / jnp.sum(vector * vector))
        vectors.append(vector)
    return jnp.stack(vectors)


def with_ends(values, stream_key, least, top_value):
    place = [jax.random.randint(jax.random.fold_in(stream_key, axis), (), 0, length) for axis, length in enumerate(values.shape)]
    widest = values.shape.index(max(values.shape))
    neighbour = place[:widest] + [(place[widest] + 1) % values.shape[widest]] + place[widest + 1:]
    return values.at[tuple(place)].set(least).at[tuple(neighbour)].set(top_value)


def shard_levels(key, shape, split, least, top_value):
    def one(axis_at, blocks):
        heights = jax.random.uniform(jax.random.fold_in(jax.random.fold_in(key, 6), axis_at), (blocks,), jnp.float32, least / len(split), top_value / len(split))
        return jnp.repeat(jnp.exp(heights), shape[axis_at] // blocks).reshape((-1,) + (1,) * (len(shape) - axis_at - 1))

    level = one(*split[0])
    for cut in split[1:]:
        level = level * one(*cut)
    return level


def noise(own_key, extent, scale, limit, cuts=(), held_as=jnp.bfloat16):
    result = jax.random.normal(own_key, extent, jnp.float32) * scale
    if len(cuts) > 0:
        result = shard_levels(own_key, extent, cuts, -0.22, 0.18) * result
    return jnp.clip(result, min=-limit, max=limit).astype(held_as)


def setup_inputs(seed: int = 0) -> dict:
    seeds = jax.random.split(jax.random.key(seed), 16)
    return {
        "positions": jnp.clip(jax.random.uniform(seeds[0], (CLUSTERS, 3, P_SIZE), jnp.float32, -1.0, 1.0) * shard_levels(seeds[0], (CLUSTERS, 3, P_SIZE), ((0, 32),), -0.4, 0.0), -1.0, 1.0),
        "normals": noise(seeds[1], (CLUSTERS, 3, P_SIZE), 0.6, 3.6, ((0, 32),), jnp.float32),
        "panel_areas": jnp.clip(jnp.exp(math.log(0.05) - 2.3025851 * jax.random.uniform(seeds[2], (CLUSTERS, P_SIZE), jnp.float32) ** shard_levels(seeds[2], (CLUSTERS, P_SIZE), ((0, 32),), -0.2, 0.2)), 0.005, 0.05),
        "panel_counts": draw_panel_counts(jax.random.fold_in(seeds[15], 71), 0),
        "near_lists": draw_near_lists(jax.random.fold_in(seeds[15], 71), 0),
        "near_counts": with_ends(jax.random.randint(seeds[5], (CLUSTERS,), 1, NNB + 1), jax.random.fold_in(seeds[5], 1), 1, NNB).astype(jnp.int32),
        "leaf_lists": draw_leaf_lists(jax.random.fold_in(seeds[15], 71), 0),
        "leaf_kinds": with_ends(jax.random.randint(seeds[7], (CLUSTERS, NIL), 0, NOP), jax.random.fold_in(seeds[7], 1), 0, NOP - 1).astype(jnp.int32),
        "group_lists": with_ends(jax.random.randint(seeds[8], (GROUPS, NIL), 0, GROUPS), jax.random.fold_in(seeds[8], 1), 0, GROUPS - 1).astype(jnp.int32),
        "group_kinds": with_ends(jax.random.randint(seeds[9], (GROUPS, NIL), 0, NOP), jax.random.fold_in(seeds[9], 1), 0, NOP - 1).astype(jnp.int32),
        "block_inverse": draw_block_inverse(jax.random.fold_in(seeds[15], 71), 0),
        "moment_maps": noise(seeds[11], (CLUSTERS, C, P_SIZE), P_SIZE ** -0.5, 0.25, ((0, 32),)),
        "up_operators": noise(seeds[12], (8, C, C), (8 * C) ** -0.5, 0.125),
        "far_operators": noise(seeds[13], (2, NOP, C, C), (C * NIL) ** -0.5, 0.09375),
        "krylov_basis": draw_krylov_basis(jax.random.fold_in(seeds[15], 71), 0),
    }


SOFTEN = 0.01
EPSILON = 1e-06
HIGH = lax.Precision.HIGHEST

def near_cluster(operands):
    target, sources = operands
    square = jnp.full((sources.shape[0], target.shape[1], sources.shape[2]), SOFTEN, jnp.float32)
    projected = jnp.zeros((sources.shape[0], target.shape[1], sources.shape[2]), jnp.float32)
    for component in range(3):
        offsets = target[component][None, :, None] - sources[:, component][:, None, :]
        square = square + offsets * offsets
        projected = projected + offsets * sources[:, 3 + component][:, None, :]
    inverse = lax.rsqrt(square)
    return lax.optimization_barrier(jnp.sum(projected * inverse * inverse * inverse, axis=(0, 2)))

def translate(chosen, kind_ids, operators):
    onehot = (kind_ids[:, :, None] == jnp.arange(operators.shape[0], dtype=jnp.int32)[None, None, :]).astype(jnp.float32)
    summed = jnp.einsum('gno,gnc->goc', onehot, chosen, precision=HIGH)
    return jnp.einsum('goc,oqc->gq', summed, operators, precision=HIGH)

def precond_one(operands):
    matrix, vector = operands
    return jnp.dot(matrix, vector, preferred_element_type=jnp.float32)

def back_one(operands):
    matrix, vector = operands
    return jnp.dot(vector, matrix, preferred_element_type=jnp.float32)

def reference(positions, normals, panel_areas, panel_counts, near_lists, near_counts, leaf_lists, leaf_kinds, group_lists, group_kinds, block_inverse, moment_maps, up_operators, far_operators, krylov_basis):
    live = (jnp.arange(P_SIZE, dtype=jnp.int32)[None, :] < panel_counts[:, None]).astype(jnp.float32)
    current = krylov_basis[KRY - 1].astype(jnp.bfloat16)
    density = (live * lax.map(precond_one, (block_inverse, current))).astype(jnp.bfloat16)
    density_wide = density.astype(jnp.float32)
    weighted = (panel_areas * density_wide)[:, None, :] * normals
    sources = jnp.concatenate([positions, weighted], axis=1)
    slot_ids = jnp.concatenate([jnp.arange(CLUSTERS, dtype=jnp.int32)[:, None], near_lists.astype(jnp.int32)], axis=1)
    slot_live = (jnp.arange(NNB + 1, dtype=jnp.int32)[None, :] <= near_counts[:, None]).astype(jnp.float32)

    def near_one(operands):
        target, slots, alive = operands
        return near_cluster((target, sources[slots] * alive[:, None, None]))
    near_field = lax.map(near_one, (positions, slot_ids, slot_live))
    moments = lax.map(precond_one, (moment_maps, density)).astype(jnp.bfloat16)
    up_wide = up_operators.astype(jnp.float32)
    far_wide = far_operators.astype(jnp.float32)
    children = moments.astype(jnp.float32).reshape(GROUPS, 8, C)
    group_moments = jnp.einsum('gkc,kqc->gq', children, up_wide, precision=HIGH)
    group_local = translate(group_moments[group_lists], group_kinds, far_wide[1]).astype(jnp.bfloat16)
    downward = jnp.einsum('gq,kqc->gkc', group_local.astype(jnp.float32), up_wide, precision=HIGH).reshape(CLUSTERS, C)
    leaf_local = (translate(moments[leaf_lists].astype(jnp.float32), leaf_kinds, far_wide[0]) + downward).astype(jnp.bfloat16)
    far_field = lax.map(back_one, (moment_maps, leaf_local))
    image = live * (0.5 * density_wide + near_field + far_field)
    entries = CLUSTERS * P_SIZE
    coeffs = jnp.einsum('kcp,cp->k', krylov_basis, image, precision=HIGH) / entries
    remainder = image - jnp.einsum('k,kcp->cp', coeffs, krylov_basis, precision=HIGH)
    height = jnp.sqrt(jnp.sum(remainder * remainder) / entries + EPSILON)
    return (remainder / height, jnp.concatenate([coeffs, height[None]]))
```

```python
import functools

import jax
import jax.numpy as jnp
from jax import lax
from jax.experimental import pallas as pl
from jax.experimental.pallas import tpu as pltpu
from jax.sharding import PartitionSpec as P

RADIUS = 3
SIDES = 2 * RADIUS + 1
SOFTEN = 0.01
EPSILON = 1e-06
JB = 256
MESH = pl.DeviceIdType.MESH
NT = (((1,), (1,)), ((), ()))
NN = (((1,), (0,)), ((), ()))
TN = (((0,), (0,)), ((), ()))
F32 = jnp.float32
BF16 = jnp.bfloat16
AXES = ("role", "dev")


def mm(a, b, dims):
    return lax.dot_general(a, b, dims, preferred_element_type=F32)


def row_is(shape, k):
    return lax.broadcasted_iota(jnp.int32, shape, 0) == k


def place(roles, devs):
    me = lax.axis_index("role") * devs + lax.axis_index("dev")
    return me, roles * devs


def coords(linear, devs):
    return (linear // devs, lax.rem(linear, devs))


def greet(me, total, devs):
    barrier = pltpu.get_barrier_semaphore()

    def body(i, carry):
        pl.semaphore_signal(
            barrier,
            inc=1,
            device_id=coords(lax.rem(me + i, total), devs),
            device_id_type=MESH,
        )
        return carry

    lax.fori_loop(1, total, body, 0)
    return barrier


def live_mask(cnt_ref, shape):
    rows = lax.broadcasted_iota(jnp.int32, shape, 0)
    limit = jnp.zeros(shape, jnp.int32)
    for c in range(shape[0]):
        limit = jnp.where(rows == c, cnt_ref[c], limit)
    return lax.broadcasted_iota(jnp.int32, shape, 1) < limit


def halves(x):
    hi = x.astype(BF16).astype(F32)
    return jnp.concatenate([hi, x - hi], axis=0).astype(BF16)


def source_kernel(
    roles,
    devs,
    cnt,
    pos,
    nrm,
    area,
    kry,
    binv,
    maps,
    ups,
    paw,
    cntw,
    densw,
    momw,
    gmall,
    binv_v,
    maps_v,
    ups_v,
    local_sem,
    big_sem,
    send_sem,
    recv_sem,
    gsend,
    grecv,
):
    me, total = place(roles, devs)
    local, panels = area.shape
    coeffs = maps_v.shape[1]
    copies = []
    for c in range(local):
        copies.append(pltpu.make_async_copy(binv.at[c], binv_v.at[c], big_sem.at[c]))
    map_copy = pltpu.make_async_copy(maps, maps_v, local_sem.at[0])
    up_copy = pltpu.make_async_copy(ups, ups_v, local_sem.at[1])
    for copy in copies:
        copy.start()
    map_copy.start()
    up_copy.start()
    barrier = greet(me, total, devs)
    for c in range(local):
        paw[RADIUS, c, 0:3, :] = pos[c]
        paw[RADIUS, c, 3:6, :] = nrm[c] * area[c : c + 1, :]
    lane = lax.broadcasted_iota(jnp.int32, (1, 128), 1)
    counts = jnp.zeros((1, 128), jnp.int32)
    for c in range(local):
        counts = jnp.where(lane == c, cnt[c], counts)
    cntw[RADIUS] = counts
    pl.semaphore_wait(barrier, total - 1)

    def to_neighbours(ref, kind):
        made = []
        for n, d in enumerate([1, -1, 2, -2, 3, -3]):
            made.append(
                pltpu.make_async_remote_copy(
                    src_ref=ref.at[RADIUS],
                    dst_ref=ref.at[RADIUS - d],
                    send_sem=send_sem.at[kind, n],
                    recv_sem=recv_sem.at[kind, n],
                    device_id=coords(lax.rem(me + d + total, total), devs),
                    device_id_type=MESH,
                )
            )
        for copy in made:
            copy.start()
        return made

    sent = to_neighbours(paw, 0) + to_neighbours(cntw, 1)
    live = live_mask(cnt, (local, panels))
    current = kry[...].astype(BF16)
    density = jnp.zeros((local, panels), F32)
    for c in range(local):
        copies[c].wait()
        found = mm(current, binv_v[c], NT)
        density = jnp.where(row_is(found.shape, c), found, density)
    rounded = jnp.where(live, density, 0.0).astype(BF16)
    densw[RADIUS] = rounded.astype(F32)
    sent += to_neighbours(densw, 2)
    map_copy.wait()
    moments = jnp.zeros((local, coeffs), F32)
    for c in range(local):
        found = mm(rounded, maps_v[c], NT)
        moments = jnp.where(row_is(found.shape, c), found, moments)
    moments = moments.astype(BF16)
    momw[RADIUS] = moments.astype(F32)
    sent += to_neighbours(momw, 3)
    up_copy.wait()
    merged = jnp.zeros((local, coeffs), F32)
    for k in range(local):
        found = mm(moments, ups_v[k], NT)
        merged = jnp.where(row_is(found.shape, k), found, merged)
    gmall[me] = jnp.sum(merged, axis=0, keepdims=True)

    def group_copy(i):
        return pltpu.make_async_remote_copy(
            src_ref=gmall.at[me],
            dst_ref=gmall.at[me],
            send_sem=gsend.at[i],
            recv_sem=grecv.at[i],
            device_id=coords(lax.rem(me + i, total), devs),
            device_id_type=MESH,
        )

    def start_one(i, carry):
        group_copy(i).start()
        return carry

    def wait_one(i, carry):
        source = lax.rem(me - i + total, total)
        pltpu.make_async_remote_copy(
            src_ref=gmall.at[me],
            dst_ref=gmall.at[source],
            send_sem=gsend.at[i],
            recv_sem=grecv.at[i],
            device_id=coords(lax.rem(me + i, total), devs),
            device_id_type=MESH,
        ).wait()
        return carry

    lax.fori_loop(1, total, start_one, 0)
    for copy in sent:
        copy.wait()
    lax.fori_loop(1, total, wait_one, 0)


def splits(x):
    hi = x.astype(BF16).astype(F32)
    rest = x - hi
    mid = rest.astype(BF16).astype(F32)
    return hi, mid, rest - mid


def near_kernel(
    first, near, used, cntw, paw, densw, out, src_sq, src_pr, feat, sq0, pr0, sq1, pr1, acc
):
    local, panels = out.shape
    chunks = panels // 128
    one = jnp.ones((1, panels), F32)
    feat[...] = jnp.zeros(feat.shape, F32)

    def cluster_body(c, carry):
        x = paw[RADIUS, c, 0:3, :]
        feat[0:3, :] = x
        feat[3:4, :] = one
        feat[4:5, :] = jnp.sum(x * x, axis=0, keepdims=True)
        hi, mid, low = splits(feat[...])
        target = jnp.concatenate([hi, mid, hi, low, hi, mid], axis=0).astype(BF16)

        def slot_body(s, offset):
            listed = near[c, jnp.maximum(s - 1, 0)] - first[0]
            w = jnp.where(s == 0, RADIUS * local + c, listed)
            side = w // local
            inner = lax.rem(w, local)
            pa = paw[side, inner]
            y = pa[0:3]
            weighted = pa[3:6] * densw[side, pl.ds(inner, 1), :]
            feat[0:3, :] = -2.0 * y
            feat[3:4, :] = jnp.sum(y * y, axis=0, keepdims=True) + SOFTEN
            feat[4:5, :] = one
            hi, mid, low = splits(feat[...])
            sq = jnp.concatenate([hi, hi, mid, hi, low, mid], axis=0).astype(BF16)
            feat[0:3, :] = weighted
            feat[3:4, :] = -jnp.sum(y * weighted, axis=0, keepdims=True)
            feat[4:5, :] = jnp.zeros_like(one)
            hi, mid, low = splits(feat[...])
            pr = jnp.concatenate([hi, hi, mid, hi, low, mid], axis=0).astype(BF16)
            count = (cntw[side, 0, inner] + 127) // 128
            for b in range(chunks):
                src_sq[offset + b] = sq[:, b * 128 : (b + 1) * 128]
                src_pr[offset + b] = pr[:, b * 128 : (b + 1) * 128]
            return offset + count

        end = lax.fori_loop(0, used[c] + 1, slot_body, 0)
        rows = lax.broadcasted_iota(jnp.int32, (48, 128), 0)
        for b in range(3):
            src_sq[end + b] = jnp.where(rows == 3, 1.0, 0.0).astype(BF16)
            src_pr[end + b] = jnp.zeros((48, 128), BF16)

        def products(block, sq_ref, pr_ref):
            for half in range(2):
                part = pl.ds(half * 128, 128)
                sq_ref[part, :] = mm(src_sq[2 * block + half], target, TN)
                pr_ref[part, :] = mm(src_pr[2 * block + half], target, TN)

        def consume(sq_ref, pr_ref):
            for r in range(0, panels, 256):
                total = acc[:, r : r + 256]
                for j in range(0, JB, 8):
                    inverse = lax.rsqrt(sq_ref[j : j + 8, r : r + 256])
                    total = total + pr_ref[j : j + 8, r : r + 256] * inverse * (
                        inverse * inverse
                    )
                acc[:, r : r + 256] = total

        acc[...] = jnp.zeros(acc.shape, F32)
        blocks = (end + 1) // 2
        products(0, sq0, pr0)

        def pair_body(t, carry):
            products(2 * t + 1, sq1, pr1)
            consume(sq0, pr0)
            products(2 * t + 2, sq0, pr0)
            consume(sq1, pr1)
            return carry

        lax.fori_loop(0, blocks // 2, pair_body, 0)

        @pl.when(lax.rem(blocks, 2) == 1)
        def _():
            consume(sq0, pr0)

        out[pl.ds(c, 1), :] = jnp.sum(acc[...], axis=0, keepdims=True)
        return carry

    lax.fori_loop(0, local, cluster_body, 0)


def finish_kernel(
    roles,
    devs,
    cnt,
    glist,
    gkind,
    llist,
    lkind,
    momw,
    gmall,
    near,
    densw,
    kry,
    maps,
    ups,
    fars,
    nxt,
    hess,
    maps_v,
    ups_v,
    fars_v,
    red,
    local_sem,
    send_sem,
    recv_sem,
):
    me, total = place(roles, devs)
    local, panels = near.shape
    coeffs = maps_v.shape[1]
    kinds = fars_v.shape[1]
    window = SIDES * local
    far_copies = [
        pltpu.make_async_copy(fars.at[level], fars_v.at[level], local_sem.at[level])
        for level in range(2)
    ]
    up_copy = pltpu.make_async_copy(ups, ups_v, local_sem.at[2])
    map_copy = pltpu.make_async_copy(maps, maps_v, local_sem.at[3])
    far_copies[1].start()
    far_copies[0].start()
    up_copy.start()
    map_copy.start()
    barrier = greet(me, total, devs)

    groups = gmall[...].reshape(total, coeffs)
    g_rows = lax.broadcasted_iota(jnp.int32, (kinds, total), 0)
    g_lanes = lax.broadcasted_iota(jnp.int32, (kinds, total), 1)
    g_hot = jnp.zeros((kinds, total), F32)
    for n in range(glist.shape[1]):
        g_hot += jnp.where((g_rows == gkind[0, n]) & (g_lanes == glist[0, n]), 1.0, 0.0)
    g_hot = g_hot.astype(BF16)
    hi, mid, low = splits(groups)
    g_sum = mm(g_hot, hi.astype(BF16), NN) + mm(g_hot, mid.astype(BF16), NN)
    g_sum += mm(g_hot, low.astype(BF16), NN)
    g_both = halves(g_sum)

    lanes = lax.broadcasted_iota(jnp.int32, (local, window), 1)
    base = (me - RADIUS) * local
    hots = [jnp.zeros((local, window), F32) for _ in range(kinds)]
    for n in range(llist.shape[1]):
        hit = lanes == (llist[:, n : n + 1] - base)
        kind = jnp.broadcast_to(lkind[:, n : n + 1], (local, window))
        for o in range(kinds):
            hots[o] = hots[o] + jnp.where(hit & (kind == o), 1.0, 0.0)
    hot = jnp.concatenate(hots, axis=0).astype(BF16)
    summed = mm(hot, momw[...].reshape(window, coeffs).astype(BF16), NN)

    far_copies[1].wait()
    g_parts = jnp.zeros((kinds, coeffs), F32)
    for o in range(kinds):
        found = mm(g_both, fars_v[1, o], NT)
        found = found[:kinds] + found[kinds:]
        g_parts = jnp.where(row_is(found.shape, o), found, g_parts)
    g_local = jnp.sum(g_parts, axis=0, keepdims=True).astype(BF16)
    far_copies[0].wait()
    leaf = jnp.zeros((local, coeffs), F32)
    for o in range(kinds):
        found = mm(halves(summed[o * local : (o + 1) * local]), fars_v[0, o], NT)
        leaf = leaf + found[:local] + found[local:]
    up_copy.wait()
    g_wide = jnp.broadcast_to(g_local.astype(F32), (local, coeffs)).astype(BF16)
    down = jnp.zeros((local, coeffs), F32)
    for k in range(local):
        found = mm(g_wide, ups_v[k], NN)
        down = jnp.where(row_is(found.shape, k), found, down)
    leaf = (leaf + down).astype(BF16)
    map_copy.wait()
    far = jnp.zeros((local, panels), F32)
    for c in range(local):
        found = mm(leaf, maps_v[c], NN)
        far = jnp.where(row_is(found.shape, c), found, far)
    live = live_mask(cnt, (local, panels))
    image = jnp.where(live, 0.5 * densw[RADIUS] + near[...] + far, 0.0)

    lane = lax.broadcasted_iota(jnp.int32, (1, 128), 1)
    count = kry.shape[0]
    row = jnp.zeros((1, 128), F32)
    for k in range(count + 1):
        part = image * (kry[k] if k < count else image)
        value = jnp.sum(jnp.sum(part, axis=0, keepdims=True), axis=1, keepdims=True)
        row = jnp.where(lane == k, value, row)
    red[me] = row
    pl.semaphore_wait(barrier, total - 1)

    def one(i):
        source = lax.rem(me - i + total, total)
        target = coords(lax.rem(me + i, total), devs)

        def copy(dst):
            return pltpu.make_async_remote_copy(
                src_ref=red.at[me],
                dst_ref=red.at[dst],
                send_sem=send_sem.at[i],
                recv_sem=recv_sem.at[i],
                device_id=target,
                device_id_type=MESH,
            )

        return copy, source

    def start_one(i, carry):
        one(i)[0](me).start()
        return carry

    def wait_one(i, carry):
        copy, source = one(i)
        copy(source).wait()
        return carry

    lax.fori_loop(1, total, start_one, 0)
    lax.fori_loop(1, total, wait_one, 0)
    scale = 1.0 / (total * local * panels)
    sums = jnp.sum(red[...], axis=0) * scale
    rest = image
    energy = sums[:, count : count + 1]
    for k in range(count):
        c_k = sums[:, k : k + 1]
        rest = rest - c_k * kry[k]
        energy = energy - c_k * c_k
    height = jnp.sqrt(energy + EPSILON)
    nxt[...] = rest / height
    hess[...] = jnp.where(lane == count, height, sums)


def shards(
    roles,
    devs,
    positions,
    normals,
    panel_areas,
    panel_counts,
    near_lists,
    near_counts,
    leaf_lists,
    leaf_kinds,
    group_lists,
    group_kinds,
    block_inverse,
    moment_maps,
    up_operators,
    far_operators,
    krylov_basis,
):
    local, _, panels = positions.shape
    coeffs = moment_maps.shape[1]
    total = roles * devs
    vmem = pl.BlockSpec(memory_space=pltpu.VMEM)
    smem = pl.BlockSpec(memory_space=pltpu.SMEM)
    hbm = pl.BlockSpec(memory_space=pl.ANY)
    dma = pltpu.SemaphoreType.DMA
    paw, cntw, densw, momw, gmall = pl.pallas_call(
        functools.partial(source_kernel, roles, devs),
        name="sources",
        out_shape=(
            jax.ShapeDtypeStruct((SIDES, local, 6, panels), F32),
            jax.ShapeDtypeStruct((SIDES, 1, 128), jnp.int32),
            jax.ShapeDtypeStruct((SIDES, local, panels), F32),
            jax.ShapeDtypeStruct((SIDES, local, coeffs), F32),
            jax.ShapeDtypeStruct((total, 1, coeffs), F32),
        ),
        in_specs=[smem, vmem, vmem, vmem, vmem, hbm, hbm, hbm],
        out_specs=(vmem,) * 5,
        scratch_shapes=[
            pltpu.VMEM(block_inverse.shape, BF16),
            pltpu.VMEM(moment_maps.shape, BF16),
            pltpu.VMEM(up_operators.shape, BF16),
            dma((2,)),
            dma((local,)),
            dma((4, 6)),
            dma((4, 6)),
            dma((total,)),
            dma((total,)),
        ],
        compiler_params=pltpu.CompilerParams(
            collective_id=0, has_side_effects=True, vmem_limit_bytes=20 << 20
        ),
    )(
        panel_counts,
        positions,
        normals,
        panel_areas,
        krylov_basis[-1],
        block_inverse,
        moment_maps,
        up_operators,
    )
    own = lax.axis_index(AXES)
    first = jnp.reshape((own - RADIUS) * local, (1,)).astype(jnp.int32)
    room = (near_lists.shape[1] + 1) * (panels // 128) + 8
    near = pl.pallas_call(
        near_kernel,
        name="near",
        out_shape=jax.ShapeDtypeStruct((local, panels), F32),
        in_specs=[smem, smem, smem, smem, vmem, vmem],
        out_specs=vmem,
        scratch_shapes=[
            pltpu.VMEM((room, 48, 128), BF16),
            pltpu.VMEM((room, 48, 128), BF16),
            pltpu.VMEM((8, panels), F32),
            pltpu.VMEM((JB, panels), F32),
            pltpu.VMEM((JB, panels), F32),
            pltpu.VMEM((JB, panels), F32),
            pltpu.VMEM((JB, panels), F32),
            pltpu.VMEM((8, panels), F32),
        ],
        compiler_params=pltpu.CompilerParams(vmem_limit_bytes=20 << 20),
    )(first, near_lists, near_counts, cntw, paw, densw)
    nxt, hess = pl.pallas_call(
        functools.partial(finish_kernel, roles, devs),
        name="finish",
        out_shape=(
            jax.ShapeDtypeStruct((local, panels), F32),
            jax.ShapeDtypeStruct((1, 128), F32),
        ),
        in_specs=[smem, smem, smem] + [vmem] * 7 + [hbm] * 3,
        out_specs=(vmem, vmem),
        scratch_shapes=[
            pltpu.VMEM(moment_maps.shape, BF16),
            pltpu.VMEM(up_operators.shape, BF16),
            pltpu.VMEM(far_operators.shape, BF16),
            pltpu.VMEM((total, 1, 128), F32),
            dma((4,)),
            dma((total,)),
            dma((total,)),
        ],
        compiler_params=pltpu.CompilerParams(
            collective_id=1, has_side_effects=True, vmem_limit_bytes=20 << 20
        ),
    )(
        panel_counts,
        group_lists,
        group_kinds,
        leaf_lists,
        leaf_kinds,
        momw,
        gmall,
        near,
        densw,
        krylov_basis,
        moment_maps,
        up_operators,
        far_operators,
    )
    return nxt, hess[0, : krylov_basis.shape[0] + 1]


def solution(mesh):
    roles, devs = mesh.shape["role"], mesh.shape["dev"]
    return jax.shard_map(
        functools.partial(shards, roles, devs),
        mesh=mesh,
        in_specs=(
            P(AXES, None, None),
            P(AXES, None, None),
            P(AXES, None),
            P(AXES),
            P(AXES, None),
            P(AXES),
            P(AXES, None),
            P(AXES, None),
            P(AXES, None),
            P(AXES, None),
            P(AXES, None, None),
            P(AXES, None, None),
            P(),
            P(),
            P(None, AXES, None),
        ),
        out_specs=(P(AXES, None), P()),
        check_vma=False,
    )
```

```python
import functools

import jax
import jax.numpy as jnp
from jax import lax
from jax.experimental import pallas as pl
from jax.experimental.pallas import tpu as pltpu
from jax.sharding import PartitionSpec as P

RADIUS = 3
SIDES = 2 * RADIUS + 1
SOFTEN = 0.01
EPSILON = 1e-06
JB = 256
MESH = pl.DeviceIdType.MESH
NT = (((1,), (1,)), ((), ()))
NN = (((1,), (0,)), ((), ()))
TN = (((0,), (0,)), ((), ()))
F32 = jnp.float32
BF16 = jnp.bfloat16
AXES = ("role", "dev")


def mm(a, b, dims):
    return lax.dot_general(a, b, dims, preferred_element_type=F32)


def row_is(shape, k):
    return lax.broadcasted_iota(jnp.int32, shape, 0) == k


def place(roles, devs):
    me = lax.axis_index("role") * devs + lax.axis_index("dev")
    return me, roles * devs


def coords(linear, devs):
    return (linear // devs, lax.rem(linear, devs))


def greet(me, total, devs):
    barrier = pltpu.get_barrier_semaphore()

    def body(i, carry):
        pl.semaphore_signal(
            barrier,
            inc=1,
            device_id=coords(lax.rem(me + i, total), devs),
            device_id_type=MESH,
        )
        return carry

    lax.fori_loop(1, total, body, 0)
    return barrier


def live_mask(cnt_ref, shape):
    rows = lax.broadcasted_iota(jnp.int32, shape, 0)
    limit = jnp.zeros(shape, jnp.int32)
    for c in range(shape[0]):
        limit = jnp.where(rows == c, cnt_ref[c], limit)
    return lax.broadcasted_iota(jnp.int32, shape, 1) < limit


def halves(x):
    hi = x.astype(BF16).astype(F32)
    return jnp.concatenate([hi, x - hi], axis=0).astype(BF16)


def source_kernel(
    roles,
    devs,
    cnt,
    pos,
    nrm,
    area,
    kry,
    binv,
    maps,
    ups,
    posw,
    anw,
    cntw,
    densw,
    momw,
    gmall,
    nrm_v,
    area_v,
    kry_v,
    binv_v,
    maps_v,
    ups_v,
    local_sem,
    big_sem,
    send_sem,
    recv_sem,
    gsend,
    grecv,
):
    me, total = place(roles, devs)
    local, panels = area.shape
    coeffs = maps_v.shape[1]
    copies = []
    for c in range(local):
        copies.append(pltpu.make_async_copy(binv.at[c], binv_v.at[c], big_sem.at[c]))
    map_copy = pltpu.make_async_copy(maps, maps_v, local_sem.at[0])
    up_copy = pltpu.make_async_copy(ups, ups_v, local_sem.at[1])
    small = [
        pltpu.make_async_copy(pos, posw.at[RADIUS], local_sem.at[2]),
        pltpu.make_async_copy(nrm, nrm_v, local_sem.at[3]),
        pltpu.make_async_copy(area, area_v, local_sem.at[4]),
        pltpu.make_async_copy(kry.at[kry.shape[0] - 1], kry_v, local_sem.at[5]),
    ]
    for copy in small + copies:
        copy.start()
    map_copy.start()
    up_copy.start()
    barrier = greet(me, total, devs)
    for copy in small:
        copy.wait()
    parts = [nrm_v[a] * area_v[...] for a in range(3)]
    anw[RADIUS] = jnp.concatenate(parts, axis=0).astype(BF16)
    lane = lax.broadcasted_iota(jnp.int32, (1, 128), 1)
    counts = jnp.zeros((1, 128), jnp.int32)
    for c in range(local):
        counts = jnp.where(lane == c, cnt[c], counts)
    cntw[RADIUS] = counts
    pl.semaphore_wait(barrier, total - 1)

    def to_neighbours(ref, kind):
        made = []
        for n, d in enumerate([1, -1, 2, -2, 3, -3]):
            made.append(
                pltpu.make_async_remote_copy(
                    src_ref=ref.at[RADIUS],
                    dst_ref=ref.at[RADIUS - d],
                    send_sem=send_sem.at[kind, n],
                    recv_sem=recv_sem.at[kind, n],
                    device_id=coords(lax.rem(me + d + total, total), devs),
                    device_id_type=MESH,
                )
            )
        for copy in made:
            copy.start()
        return made

    sent = to_neighbours(posw, 0) + to_neighbours(anw, 4) + to_neighbours(cntw, 1)
    live = live_mask(cnt, (local, panels))
    current = kry_v[...].astype(BF16)
    density = jnp.zeros((local, panels), F32)
    for c in range(local):
        copies[c].wait()
        found = mm(current, binv_v[c], NT)
        density = jnp.where(row_is(found.shape, c), found, density)
    rounded = jnp.where(live, density, 0.0).astype(BF16)
    densw[RADIUS] = rounded
    sent += to_neighbours(densw, 2)
    map_copy.wait()
    moments = jnp.zeros((local, coeffs), F32)
    for c in range(local):
        found = mm(rounded, maps_v[c], NT)
        moments = jnp.where(row_is(found.shape, c), found, moments)
    moments = moments.astype(BF16)
    momw[RADIUS] = moments
    sent += to_neighbours(momw, 3)
    up_copy.wait()
    merged = jnp.zeros((local, coeffs), F32)
    for k in range(local):
        found = mm(moments, ups_v[k], NT)
        merged = jnp.where(row_is(found.shape, k), found, merged)
    gmall[me] = jnp.sum(merged, axis=0, keepdims=True)

    def group_copy(i):
        return pltpu.make_async_remote_copy(
            src_ref=gmall.at[me],
            dst_ref=gmall.at[me],
            send_sem=gsend.at[i],
            recv_sem=grecv.at[i],
            device_id=coords(lax.rem(me + i, total), devs),
            device_id_type=MESH,
        )

    def start_one(i, carry):
        group_copy(i).start()
        return carry

    def wait_one(i, carry):
        source = lax.rem(me - i + total, total)
        pltpu.make_async_remote_copy(
            src_ref=gmall.at[me],
            dst_ref=gmall.at[source],
            send_sem=gsend.at[i],
            recv_sem=grecv.at[i],
            device_id=coords(lax.rem(me + i, total), devs),
            device_id_type=MESH,
        ).wait()
        return carry

    lax.fori_loop(1, total, start_one, 0)
    for copy in sent:
        copy.wait()
    lax.fori_loop(1, total, wait_one, 0)


def splits(x):
    hi = x.astype(BF16).astype(F32)
    rest = x - hi
    mid = rest.astype(BF16).astype(F32)
    return hi, mid, rest - mid


def near_kernel(
    first, near, used, cntw, posw, anw, densw, out, src_sq, src_pr, weight, sq0, pr0, sq1, pr1, acc
):
    local, panels = out.shape
    chunks = panels // 128
    shape = (8, panels)
    rows = lax.broadcasted_iota(jnp.int32, shape, 0)
    for side in range(SIDES):
        dens = densw[side].astype(F32)
        products_an = anw[side].astype(F32)
        for a in range(3):
            weight[side, a] = products_an[a * local : (a + 1) * local] * dens

    def vectors(ref, side, inner):
        return [
            jnp.broadcast_to(ref[side, a, pl.ds(inner, 1), :], shape) for a in range(3)
        ]

    def stack(values):
        feat = jnp.zeros(shape, F32)
        for k, value in enumerate(values):
            feat = jnp.where(rows == k, value, feat)
        return feat

    def pack(feat, order):
        parts = splits(feat)
        return jnp.concatenate([parts[k] for k in order], axis=0).astype(BF16)

    def cluster_body(c, carry):
        x0, x1, x2 = vectors(posw, RADIUS, c)
        norm = x0 * x0 + x1 * x1 + x2 * x2
        target = pack(stack([x0, x1, x2, 1.0, norm]), (0, 1, 0, 2, 0, 1))

        def slot_body(s, offset):
            listed = near[c, jnp.maximum(s - 1, 0)] - first[0]
            w = jnp.where(s == 0, RADIUS * local + c, listed)
            side = w // local
            inner = lax.rem(w, local)
            y0, y1, y2 = vectors(posw, side, inner)
            w0, w1, w2 = vectors(weight, side, inner)
            norm = y0 * y0 + y1 * y1 + y2 * y2 + SOFTEN
            inside = -(y0 * w0 + y1 * w1 + y2 * w2)
            order = (0, 0, 1, 0, 2, 1)
            sq = pack(stack([-2.0 * y0, -2.0 * y1, -2.0 * y2, norm, 1.0]), order)
            pr = pack(stack([w0, w1, w2, inside]), order)
            count = (cntw[side, 0, inner] + 127) // 128
            for b in range(chunks):
                src_sq[offset + b] = sq[:, b * 128 : (b + 1) * 128]
                src_pr[offset + b] = pr[:, b * 128 : (b + 1) * 128]
            return offset + count

        end = lax.fori_loop(0, used[c] + 1, slot_body, 0)
        pad_rows = lax.broadcasted_iota(jnp.int32, (48, 128), 0)
        for b in range(3):
            src_sq[end + b] = jnp.where(pad_rows == 3, 1.0, 0.0).astype(BF16)
            src_pr[end + b] = jnp.zeros((48, 128), BF16)

        def products(block, sq_ref, pr_ref):
            for half in range(2):
                part = pl.ds(half * 128, 128)
                sq_ref[part, :] = mm(src_sq[2 * block + half], target, TN)
                pr_ref[part, :] = mm(src_pr[2 * block + half], target, TN)

        def consume(sq_ref, pr_ref):
            for r in range(0, panels, 256):
                total = acc[:, r : r + 256]
                for j in range(0, JB, 8):
                    inverse = lax.rsqrt(sq_ref[j : j + 8, r : r + 256])
                    total = total + pr_ref[j : j + 8, r : r + 256] * inverse * (
                        inverse * inverse
                    )
                acc[:, r : r + 256] = total

        acc[...] = jnp.zeros(acc.shape, F32)
        blocks = (end + 1) // 2
        products(0, sq0, pr0)

        def pair_body(t, carry):
            products(2 * t + 1, sq1, pr1)
            consume(sq0, pr0)
            products(2 * t + 2, sq0, pr0)
            consume(sq1, pr1)
            return carry

        lax.fori_loop(0, blocks // 2, pair_body, 0)

        @pl.when(lax.rem(blocks, 2) == 1)
        def _():
            consume(sq0, pr0)

        out[pl.ds(c, 1), :] = jnp.sum(acc[...], axis=0, keepdims=True)
        return carry

    lax.fori_loop(0, local, cluster_body, 0)


def finish_kernel(
    roles,
    devs,
    cnt,
    glist,
    gkind,
    llist,
    lkind,
    momw,
    gmall,
    near,
    densw,
    kry,
    maps_v,
    ups_v,
    fars_v,
    nxt,
    hess,
    red,
    send_sem,
    recv_sem,
):
    me, total = place(roles, devs)
    local, panels = near.shape
    coeffs = maps_v.shape[1]
    kinds = fars_v.shape[1]
    window = SIDES * local
    barrier = greet(me, total, devs)

    groups = gmall[...].reshape(total, coeffs)
    g_rows = lax.broadcasted_iota(jnp.int32, (kinds, total), 0)
    g_lanes = lax.broadcasted_iota(jnp.int32, (kinds, total), 1)
    g_hot = jnp.zeros((kinds, total), F32)
    for n in range(glist.shape[1]):
        g_hot += jnp.where((g_rows == gkind[0, n]) & (g_lanes == glist[0, n]), 1.0, 0.0)
    g_hot = g_hot.astype(BF16)
    hi, mid, low = splits(groups)
    g_sum = mm(g_hot, hi.astype(BF16), NN) + mm(g_hot, mid.astype(BF16), NN)
    g_sum += mm(g_hot, low.astype(BF16), NN)
    g_both = halves(g_sum)

    lanes = lax.broadcasted_iota(jnp.int32, (local, window), 1)
    base = (me - RADIUS) * local
    hots = [jnp.zeros((local, window), F32) for _ in range(kinds)]
    for n in range(llist.shape[1]):
        hit = lanes == (llist[:, n : n + 1] - base)
        kind = jnp.broadcast_to(lkind[:, n : n + 1], (local, window))
        for o in range(kinds):
            hots[o] = hots[o] + jnp.where(hit & (kind == o), 1.0, 0.0)
    hot = jnp.concatenate(hots, axis=0).astype(BF16)
    held = jnp.concatenate([momw[side].astype(F32) for side in range(SIDES)], axis=0)
    summed = mm(hot, held.astype(BF16), NN)

    g_parts = jnp.zeros((kinds, coeffs), F32)
    for o in range(kinds):
        found = mm(g_both, fars_v[1, o], NT)
        found = found[:kinds] + found[kinds:]
        g_parts = jnp.where(row_is(found.shape, o), found, g_parts)
    g_local = jnp.sum(g_parts, axis=0, keepdims=True).astype(BF16)
    leaf = jnp.zeros((local, coeffs), F32)
    for o in range(kinds):
        found = mm(halves(summed[o * local : (o + 1) * local]), fars_v[0, o], NT)
        leaf = leaf + found[:local] + found[local:]
    g_wide = jnp.broadcast_to(g_local.astype(F32), (local, coeffs)).astype(BF16)
    down = jnp.zeros((local, coeffs), F32)
    for k in range(local):
        found = mm(g_wide, ups_v[k], NN)
        down = jnp.where(row_is(found.shape, k), found, down)
    leaf = (leaf + down).astype(BF16)
    far = jnp.zeros((local, panels), F32)
    for c in range(local):
        found = mm(leaf, maps_v[c], NN)
        far = jnp.where(row_is(found.shape, c), found, far)
    live = live_mask(cnt, (local, panels))
    image = jnp.where(live, 0.5 * densw[RADIUS].astype(F32) + near[...] + far, 0.0)

    lane = lax.broadcasted_iota(jnp.int32, (1, 128), 1)
    count = kry.shape[0]
    row = jnp.zeros((1, 128), F32)
    for k in range(count + 1):
        part = image * (kry[k] if k < count else image)
        value = jnp.sum(jnp.sum(part, axis=0, keepdims=True), axis=1, keepdims=True)
        row = jnp.where(lane == k, value, row)
    red[me] = row
    pl.semaphore_wait(barrier, total - 1)

    def one(i):
        source = lax.rem(me - i + total, total)
        target = coords(lax.rem(me + i, total), devs)

        def copy(dst):
            return pltpu.make_async_remote_copy(
                src_ref=red.at[me],
                dst_ref=red.at[dst],
                send_sem=send_sem.at[i],
                recv_sem=recv_sem.at[i],
                device_id=target,
                device_id_type=MESH,
            )

        return copy, source

    def start_one(i, carry):
        one(i)[0](me).start()
        return carry

    def wait_one(i, carry):
        copy, source = one(i)
        copy(source).wait()
        return carry

    lax.fori_loop(1, total, start_one, 0)
    lax.fori_loop(1, total, wait_one, 0)
    scale = 1.0 / (total * local * panels)
    sums = jnp.sum(red[...], axis=0) * scale
    rest = image
    energy = sums[:, count : count + 1]
    for k in range(count):
        c_k = sums[:, k : k + 1]
        rest = rest - c_k * kry[k]
        energy = energy - c_k * c_k
    height = jnp.sqrt(energy + EPSILON)
    nxt[...] = rest / height
    hess[...] = jnp.where(lane == count, height, sums)[:, : count + 1]


def shards(
    roles,
    devs,
    positions,
    normals,
    panel_areas,
    panel_counts,
    near_lists,
    near_counts,
    leaf_lists,
    leaf_kinds,
    group_lists,
    group_kinds,
    block_inverse,
    moment_maps,
    up_operators,
    far_operators,
    krylov_basis,
):
    local, _, panels = positions.shape
    coeffs = moment_maps.shape[1]
    total = roles * devs
    vmem = pl.BlockSpec(memory_space=pltpu.VMEM)
    smem = pl.BlockSpec(memory_space=pltpu.SMEM)
    hbm = pl.BlockSpec(memory_space=pltpu.HBM)
    dma = pltpu.SemaphoreType.DMA
    posw, anw, cntw, densw, momw, gmall = pl.pallas_call(
        functools.partial(source_kernel, roles, devs),
        name="sources",
        out_shape=(
            jax.ShapeDtypeStruct((SIDES, 3, local, panels), F32),
            jax.ShapeDtypeStruct((SIDES, 3 * local, panels), BF16),
            jax.ShapeDtypeStruct((SIDES, 1, 128), jnp.int32),
            jax.ShapeDtypeStruct((SIDES, local, panels), BF16),
            jax.ShapeDtypeStruct((SIDES, local, coeffs), BF16),
            jax.ShapeDtypeStruct((total, 1, coeffs), F32),
        ),
        in_specs=[smem] + [hbm] * 7,
        out_specs=(vmem,) * 6,
        scratch_shapes=[
            pltpu.VMEM((3, local, panels), F32),
            pltpu.VMEM((local, panels), F32),
            pltpu.VMEM((local, panels), F32),
            pltpu.VMEM(block_inverse.shape, BF16),
            pltpu.VMEM(moment_maps.shape, BF16),
            pltpu.VMEM(up_operators.shape, BF16),
            dma((6,)),
            dma((local,)),
            dma((5, 6)),
            dma((5, 6)),
            dma((total,)),
            dma((total,)),
        ],
        compiler_params=pltpu.CompilerParams(
            collective_id=0, has_side_effects=True, vmem_limit_bytes=62 << 20
        ),
    )(
        panel_counts,
        jnp.transpose(positions, (1, 0, 2)),
        jnp.transpose(normals, (1, 0, 2)),
        panel_areas,
        krylov_basis,
        block_inverse,
        moment_maps,
        up_operators,
    )
    own = lax.axis_index(AXES)
    first = jnp.reshape((own - RADIUS) * local, (1,)).astype(jnp.int32)
    room = (near_lists.shape[1] + 1) * (panels // 128) + 8
    near = pl.pallas_call(
        near_kernel,
        name="near",
        cost_estimate=pl.CostEstimate(
            flops=40 * local * panels * panels * (near_lists.shape[1] + 1),
            bytes_accessed=48 * local * panels * SIDES,
            transcendentals=local * panels * panels * (near_lists.shape[1] + 1),
        ),
        out_shape=jax.ShapeDtypeStruct((local, panels), F32),
        in_specs=[smem, smem, smem, smem, vmem, vmem, vmem],
        out_specs=vmem,
        scratch_shapes=[
            pltpu.VMEM((room, 48, 128), BF16),
            pltpu.VMEM((room, 48, 128), BF16),
            pltpu.VMEM((SIDES, 3, local, panels), F32),
            pltpu.VMEM((JB, panels), F32),
            pltpu.VMEM((JB, panels), F32),
            pltpu.VMEM((JB, panels), F32),
            pltpu.VMEM((JB, panels), F32),
            pltpu.VMEM((8, panels), F32),
        ],
        compiler_params=pltpu.CompilerParams(vmem_limit_bytes=10 << 20),
    )(first, near_lists, near_counts, cntw, posw, anw, densw)
    nxt, hess = pl.pallas_call(
        functools.partial(finish_kernel, roles, devs),
        name="finish",
        out_shape=(
            jax.ShapeDtypeStruct((local, panels), F32),
            jax.ShapeDtypeStruct((1, krylov_basis.shape[0] + 1), F32),
        ),
        in_specs=[smem, smem, smem] + [vmem] * 10,
        out_specs=(vmem, vmem),
        scratch_shapes=[
            pltpu.VMEM((total, 1, 128), F32),
            dma((total,)),
            dma((total,)),
        ],
        compiler_params=pltpu.CompilerParams(
            collective_id=1, has_side_effects=True, vmem_limit_bytes=14 << 20
        ),
    )(
        panel_counts,
        group_lists,
        group_kinds,
        leaf_lists,
        leaf_kinds,
        momw,
        gmall,
        near,
        densw,
        krylov_basis,
        moment_maps,
        up_operators,
        far_operators,
    )
    return nxt, jnp.reshape(hess, (krylov_basis.shape[0] + 1,))


def solution(mesh):
    roles, devs = mesh.shape["role"], mesh.shape["dev"]
    return jax.shard_map(
        functools.partial(shards, roles, devs),
        mesh=mesh,
        in_specs=(
            P(AXES, None, None),
            P(AXES, None, None),
            P(AXES, None),
            P(AXES),
            P(AXES, None),
            P(AXES),
            P(AXES, None),
            P(AXES, None),
            P(AXES, None),
            P(AXES, None),
            P(AXES, None, None),
            P(AXES, None, None),
            P(),
            P(),
            P(None, AXES, None),
        ),
        out_specs=(P(AXES, None), P()),
        check_vma=False,
    )
```

```python
import functools

import jax
import jax.numpy as jnp
from jax import lax
from jax.experimental import pallas as pl
from jax.experimental.pallas import tpu as pltpu
from jax.sharding import PartitionSpec as P

RADIUS = 3
SIDES = 2 * RADIUS + 1
SOFTEN = 0.01
EPSILON = 1e-06
JB = 256
MESH = pl.DeviceIdType.MESH
NT = (((1,), (1,)), ((), ()))
NN = (((1,), (0,)), ((), ()))
TN = (((0,), (0,)), ((), ()))
F32 = jnp.float32
BF16 = jnp.bfloat16
AXES = ("role", "dev")


def mm(a, b, dims):
    return lax.dot_general(a, b, dims, preferred_element_type=F32)


def row_is(shape, k):
    return lax.broadcasted_iota(jnp.int32, shape, 0) == k


def place(roles, devs):
    me = lax.axis_index("role") * devs + lax.axis_index("dev")
    return me, roles * devs


def coords(linear, devs):
    return (linear // devs, lax.rem(linear, devs))


def greet(me, total, devs):
    barrier = pltpu.get_barrier_semaphore()

    def body(i, carry):
        pl.semaphore_signal(
            barrier,
            inc=1,
            device_id=coords(lax.rem(me + i, total), devs),
            device_id_type=MESH,
        )
        return carry

    lax.fori_loop(1, total, body, 0)
    return barrier


def live_mask(cnt_ref, shape):
    rows = lax.broadcasted_iota(jnp.int32, shape, 0)
    limit = jnp.zeros(shape, jnp.int32)
    for c in range(shape[0]):
        limit = jnp.where(rows == c, cnt_ref[c], limit)
    return lax.broadcasted_iota(jnp.int32, shape, 1) < limit


def halves(x):
    hi = x.astype(BF16).astype(F32)
    return jnp.concatenate([hi, x - hi], axis=0).astype(BF16)


def source_kernel(
    roles,
    devs,
    cnt,
    pos,
    nrm,
    area,
    kry,
    binv,
    maps,
    ups,
    posw,
    anw,
    cntw,
    densw,
    momw,
    gmall,
    nrm_v,
    area_v,
    kry_v,
    binv_v,
    maps_v,
    ups_v,
    local_sem,
    big_sem,
    send_sem,
    recv_sem,
    gsend,
    grecv,
):
    me, total = place(roles, devs)
    local, panels = area.shape
    coeffs = maps_v.shape[1]
    copies = []
    for c in range(local):
        copies.append(pltpu.make_async_copy(binv.at[c], binv_v.at[c], big_sem.at[c]))
    map_copy = pltpu.make_async_copy(maps, maps_v, local_sem.at[0])
    up_copy = pltpu.make_async_copy(ups, ups_v, local_sem.at[1])
    small = [
        pltpu.make_async_copy(pos, posw.at[RADIUS], local_sem.at[2]),
        pltpu.make_async_copy(nrm, nrm_v, local_sem.at[3]),
        pltpu.make_async_copy(area, area_v, local_sem.at[4]),
        pltpu.make_async_copy(kry.at[kry.shape[0] - 1], kry_v, local_sem.at[5]),
    ]
    for copy in small + copies:
        copy.start()
    map_copy.start()
    up_copy.start()
    barrier = greet(me, total, devs)
    for copy in small:
        copy.wait()
    parts = [nrm_v[a] * area_v[...] for a in range(3)]
    anw[RADIUS] = jnp.concatenate(parts, axis=0).astype(BF16)
    lane = lax.broadcasted_iota(jnp.int32, (1, 128), 1)
    counts = jnp.zeros((1, 128), jnp.int32)
    for c in range(local):
        counts = jnp.where(lane == c, cnt[c], counts)
    cntw[RADIUS] = counts
    pl.semaphore_wait(barrier, total - 1)

    def to_neighbours(ref, kind):
        made = []
        for n, d in enumerate([1, -1, 2, -2, 3, -3]):
            made.append(
                pltpu.make_async_remote_copy(
                    src_ref=ref.at[RADIUS],
                    dst_ref=ref.at[RADIUS - d],
                    send_sem=send_sem.at[kind, n],
                    recv_sem=recv_sem.at[kind, n],
                    device_id=coords(lax.rem(me + d + total, total), devs),
                    device_id_type=MESH,
                )
            )
        for copy in made:
            copy.start()
        return made

    sent = to_neighbours(posw, 0) + to_neighbours(anw, 4) + to_neighbours(cntw, 1)
    live = live_mask(cnt, (local, panels))
    current = kry_v[...].astype(BF16)
    density = jnp.zeros((local, panels), F32)
    for c in range(local):
        copies[c].wait()
        found = mm(current, binv_v[c], NT)
        density = jnp.where(row_is(found.shape, c), found, density)
    rounded = jnp.where(live, density, 0.0).astype(BF16)
    densw[RADIUS] = rounded
    sent += to_neighbours(densw, 2)
    map_copy.wait()
    moments = jnp.zeros((local, coeffs), F32)
    for c in range(local):
        found = mm(rounded, maps_v[c], NT)
        moments = jnp.where(row_is(found.shape, c), found, moments)
    moments = moments.astype(BF16)
    momw[RADIUS] = moments
    sent += to_neighbours(momw, 3)
    up_copy.wait()
    merged = jnp.zeros((local, coeffs), F32)
    for k in range(local):
        found = mm(moments, ups_v[k], NT)
        merged = jnp.where(row_is(found.shape, k), found, merged)
    gmall[me] = jnp.sum(merged, axis=0, keepdims=True)

    def group_copy(i):
        return pltpu.make_async_remote_copy(
            src_ref=gmall.at[me],
            dst_ref=gmall.at[me],
            send_sem=gsend.at[i],
            recv_sem=grecv.at[i],
            device_id=coords(lax.rem(me + i, total), devs),
            device_id_type=MESH,
        )

    def start_one(i, carry):
        group_copy(i).start()
        return carry

    def wait_one(i, carry):
        source = lax.rem(me - i + total, total)
        pltpu.make_async_remote_copy(
            src_ref=gmall.at[me],
            dst_ref=gmall.at[source],
            send_sem=gsend.at[i],
            recv_sem=grecv.at[i],
            device_id=coords(lax.rem(me + i, total), devs),
            device_id_type=MESH,
        ).wait()
        return carry

    lax.fori_loop(1, total, start_one, 0)
    for copy in sent:
        copy.wait()
    lax.fori_loop(1, total, wait_one, 0)


def splits(x):
    hi = x.astype(BF16).astype(F32)
    rest = x - hi
    mid = rest.astype(BF16).astype(F32)
    return hi, mid, rest - mid


def near_kernel(
    first, near, used, cntw, posw, anw, densw, out, src_sq, src_pr, weight, target_v, result, sq0, pr0, sq1, pr1, acc
):
    local, panels = out.shape
    chunks = panels // 128
    shape = (8, panels)
    rows = lax.broadcasted_iota(jnp.int32, shape, 0)
    for side in range(SIDES):
        dens = densw[side].astype(F32)
        products_an = anw[side].astype(F32)
        for a in range(3):
            weight[side, a] = products_an[a * local : (a + 1) * local] * dens

    def vectors(ref, side, inner):
        return [
            jnp.broadcast_to(ref[side, a, pl.ds(inner, 1), :], shape) for a in range(3)
        ]

    def stack(values):
        feat = jnp.zeros(shape, F32)
        for k, value in enumerate(values):
            feat = jnp.where(rows == k, value, feat)
        return feat

    def pack(feat, order):
        parts = splits(feat)
        return jnp.concatenate([parts[k] for k in order], axis=0).astype(BF16)

    def cluster_body(c, carry):
        x0, x1, x2 = vectors(posw, RADIUS, c)
        norm = x0 * x0 + x1 * x1 + x2 * x2
        target = pack(stack([x0, x1, x2, 1.0, norm]), (0, 1, 0, 2, 0, 1))

        def slot_body(s, offset):
            listed = near[c, jnp.maximum(s - 1, 0)] - first[0]
            w = jnp.where(s == 0, RADIUS * local + c, listed)
            side = w // local
            inner = lax.rem(w, local)
            y0, y1, y2 = vectors(posw, side, inner)
            w0, w1, w2 = vectors(weight, side, inner)
            norm = y0 * y0 + y1 * y1 + y2 * y2 + SOFTEN
            inside = -(y0 * w0 + y1 * w1 + y2 * w2)
            order = (0, 0, 1, 0, 2, 1)
            sq = pack(stack([-2.0 * y0, -2.0 * y1, -2.0 * y2, norm, 1.0]), order)
            pr = pack(stack([w0, w1, w2, inside]), order)
            count = (cntw[side, 0, inner] + 127) // 128
            for b in range(chunks):
                src_sq[offset + b] = sq[:, b * 128 : (b + 1) * 128]
                src_pr[offset + b] = pr[:, b * 128 : (b + 1) * 128]
            return offset + count

        end = lax.fori_loop(0, used[c] + 1, slot_body, 0)
        pad_rows = lax.broadcasted_iota(jnp.int32, (48, 128), 0)
        for b in range(3):
            src_sq[end + b] = jnp.where(pad_rows == 3, 1.0, 0.0).astype(BF16)
            src_pr[end + b] = jnp.zeros((48, 128), BF16)

        blocks = (end + 1) // 2
        wide = target_v.shape[2]
        for h in range(target_v.shape[0]):
            target_v[h] = target[:, h * wide : (h + 1) * wide]

        def half_body(h, carry):
            aim = target_v[h]

            def products(block, sq_ref, pr_ref):
                for half in range(2):
                    part = pl.ds(half * 128, 128)
                    sq_ref[part, :] = mm(src_sq[2 * block + half], aim, TN)
                    pr_ref[part, :] = mm(src_pr[2 * block + half], aim, TN)

            def consume(sq_ref, pr_ref):
                total = acc[...]
                for j in range(0, JB, 8):
                    inverse = lax.rsqrt(sq_ref[j : j + 8, :])
                    total = total + pr_ref[j : j + 8, :] * inverse * (inverse * inverse)
                acc[...] = total

            acc[...] = jnp.zeros(acc.shape, F32)
            products(0, sq0, pr0)

            def pair_body(t, inner_carry):
                products(2 * t + 1, sq1, pr1)
                consume(sq0, pr0)
                products(2 * t + 2, sq0, pr0)
                consume(sq1, pr1)
                return inner_carry

            lax.fori_loop(0, blocks // 2, pair_body, 0)

            @pl.when(lax.rem(blocks, 2) == 1)
            def _():
                consume(sq0, pr0)

            result[h, pl.ds(c, 1), :] = jnp.sum(acc[...], axis=0, keepdims=True)
            return carry

        lax.fori_loop(0, (cntw[RADIUS, 0, c] + wide - 1) // wide, half_body, 0)
        return carry

    result[...] = jnp.zeros(result.shape, F32)
    lax.fori_loop(0, local, cluster_body, 0)
    for h in range(result.shape[0]):
        wide = result.shape[2]
        out[:, h * wide : (h + 1) * wide] = result[h]


def finish_kernel(
    roles,
    devs,
    cnt,
    glist,
    gkind,
    llist,
    lkind,
    momw,
    gmall,
    near,
    densw,
    kry,
    maps_v,
    ups_v,
    fars_v,
    nxt,
    hess,
    red,
    send_sem,
    recv_sem,
):
    me, total = place(roles, devs)
    local, panels = near.shape
    coeffs = maps_v.shape[1]
    kinds = fars_v.shape[1]
    window = SIDES * local
    barrier = greet(me, total, devs)

    groups = gmall[...].reshape(total, coeffs)
    g_rows = lax.broadcasted_iota(jnp.int32, (kinds, total), 0)
    g_lanes = lax.broadcasted_iota(jnp.int32, (kinds, total), 1)
    g_hot = jnp.zeros((kinds, total), F32)
    for n in range(glist.shape[1]):
        g_hot += jnp.where((g_rows == gkind[0, n]) & (g_lanes == glist[0, n]), 1.0, 0.0)
    g_hot = g_hot.astype(BF16)
    hi, mid, low = splits(groups)
    g_sum = mm(g_hot, hi.astype(BF16), NN) + mm(g_hot, mid.astype(BF16), NN)
    g_sum += mm(g_hot, low.astype(BF16), NN)
    g_both = halves(g_sum)

    lanes = lax.broadcasted_iota(jnp.int32, (local, window), 1)
    base = (me - RADIUS) * local
    hots = [jnp.zeros((local, window), F32) for _ in range(kinds)]
    for n in range(llist.shape[1]):
        hit = lanes == (llist[:, n : n + 1] - base)
        kind = jnp.broadcast_to(lkind[:, n : n + 1], (local, window))
        for o in range(kinds):
            hots[o] = hots[o] + jnp.where(hit & (kind == o), 1.0, 0.0)
    hot = jnp.concatenate(hots, axis=0).astype(BF16)
    held = jnp.concatenate([momw[side].astype(F32) for side in range(SIDES)], axis=0)
    summed = mm(hot, held.astype(BF16), NN)

    g_parts = jnp.zeros((kinds, coeffs), F32)
    for o in range(kinds):
        found = mm(g_both, fars_v[1, o], NT)
        found = found[:kinds] + found[kinds:]
        g_parts = jnp.where(row_is(found.shape, o), found, g_parts)
    g_local = jnp.sum(g_parts, axis=0, keepdims=True).astype(BF16)
    leaf = jnp.zeros((local, coeffs), F32)
    for o in range(kinds):
        found = mm(halves(summed[o * local : (o + 1) * local]), fars_v[0, o], NT)
        leaf = leaf + found[:local] + found[local:]
    g_wide = jnp.broadcast_to(g_local.astype(F32), (local, coeffs)).astype(BF16)
    down = jnp.zeros((local, coeffs), F32)
    for k in range(local):
        found = mm(g_wide, ups_v[k], NN)
        down = jnp.where(row_is(found.shape, k), found, down)
    leaf = (leaf + down).astype(BF16)
    far = jnp.zeros((local, panels), F32)
    for c in range(local):
        found = mm(leaf, maps_v[c], NN)
        far = jnp.where(row_is(found.shape, c), found, far)
    live = live_mask(cnt, (local, panels))
    image = jnp.where(live, 0.5 * densw[RADIUS].astype(F32) + near[...] + far, 0.0)

    lane = lax.broadcasted_iota(jnp.int32, (1, 128), 1)
    count = kry.shape[0]
    row = jnp.zeros((1, 128), F32)
    for k in range(count + 1):
        part = image * (kry[k] if k < count else image)
        value = jnp.sum(jnp.sum(part, axis=0, keepdims=True), axis=1, keepdims=True)
        row = jnp.where(lane == k, value, row)
    red[me] = row
    pl.semaphore_wait(barrier, total - 1)

    def one(i):
        source = lax.rem(me - i + total, total)
        target = coords(lax.rem(me + i, total), devs)

        def copy(dst):
            return pltpu.make_async_remote_copy(
                src_ref=red.at[me],
                dst_ref=red.at[dst],
                send_sem=send_sem.at[i],
                recv_sem=recv_sem.at[i],
                device_id=target,
                device_id_type=MESH,
            )

        return copy, source

    def start_one(i, carry):
        one(i)[0](me).start()
        return carry

    def wait_one(i, carry):
        copy, source = one(i)
        copy(source).wait()
        return carry

    lax.fori_loop(1, total, start_one, 0)
    lax.fori_loop(1, total, wait_one, 0)
    scale = 1.0 / (total * local * panels)
    sums = jnp.sum(red[...], axis=0) * scale
    rest = image
    energy = sums[:, count : count + 1]
    for k in range(count):
        c_k = sums[:, k : k + 1]
        rest = rest - c_k * kry[k]
        energy = energy - c_k * c_k
    height = jnp.sqrt(energy + EPSILON)
    nxt[...] = rest / height
    hess[...] = jnp.where(lane == count, height, sums)[:, : count + 1]


def shards(
    roles,
    devs,
    positions,
    normals,
    panel_areas,
    panel_counts,
    near_lists,
    near_counts,
    leaf_lists,
    leaf_kinds,
    group_lists,
    group_kinds,
    block_inverse,
    moment_maps,
    up_operators,
    far_operators,
    krylov_basis,
):
    local, _, panels = positions.shape
    coeffs = moment_maps.shape[1]
    total = roles * devs
    vmem = pl.BlockSpec(memory_space=pltpu.VMEM)
    smem = pl.BlockSpec(memory_space=pltpu.SMEM)
    hbm = pl.BlockSpec(memory_space=pltpu.HBM)
    dma = pltpu.SemaphoreType.DMA
    posw, anw, cntw, densw, momw, gmall = pl.pallas_call(
        functools.partial(source_kernel, roles, devs),
        name="sources",
        out_shape=(
            jax.ShapeDtypeStruct((SIDES, 3, local, panels), F32),
            jax.ShapeDtypeStruct((SIDES, 3 * local, panels), BF16),
            jax.ShapeDtypeStruct((SIDES, 1, 128), jnp.int32),
            jax.ShapeDtypeStruct((SIDES, local, panels), BF16),
            jax.ShapeDtypeStruct((SIDES, local, coeffs), BF16),
            jax.ShapeDtypeStruct((total, 1, coeffs), F32),
        ),
        in_specs=[smem] + [hbm] * 7,
        out_specs=(vmem,) * 6,
        scratch_shapes=[
            pltpu.VMEM((3, local, panels), F32),
            pltpu.VMEM((local, panels), F32),
            pltpu.VMEM((local, panels), F32),
            pltpu.VMEM(block_inverse.shape, BF16),
            pltpu.VMEM(moment_maps.shape, BF16),
            pltpu.VMEM(up_operators.shape, BF16),
            dma((6,)),
            dma((local,)),
            dma((5, 6)),
            dma((5, 6)),
            dma((total,)),
            dma((total,)),
        ],
        compiler_params=pltpu.CompilerParams(
            collective_id=0, has_side_effects=True, vmem_limit_bytes=62 << 20
        ),
    )(
        panel_counts,
        jnp.transpose(positions, (1, 0, 2)),
        jnp.transpose(normals, (1, 0, 2)),
        panel_areas,
        krylov_basis,
        block_inverse,
        moment_maps,
        up_operators,
    )
    own = lax.axis_index(AXES)
    first = jnp.reshape((own - RADIUS) * local, (1,)).astype(jnp.int32)
    wide = min(256, panels)
    room = (near_lists.shape[1] + 1) * (panels // 128) + 8
    near = pl.pallas_call(
        near_kernel,
        name="near",
        cost_estimate=pl.CostEstimate(
            flops=40 * local * panels * panels * (near_lists.shape[1] + 1),
            bytes_accessed=48 * local * panels * SIDES,
            transcendentals=local * panels * panels * (near_lists.shape[1] + 1),
        ),
        out_shape=jax.ShapeDtypeStruct((local, panels), F32),
        in_specs=[smem, smem, smem, smem, vmem, vmem, vmem],
        out_specs=vmem,
        scratch_shapes=[
            pltpu.VMEM((room, 48, 128), BF16),
            pltpu.VMEM((room, 48, 128), BF16),
            pltpu.VMEM((SIDES, 3, local, panels), F32),
            pltpu.VMEM((panels // wide, 48, wide), BF16),
            pltpu.VMEM((panels // wide, local, wide), F32),
            pltpu.VMEM((JB, wide), F32),
            pltpu.VMEM((JB, wide), F32),
            pltpu.VMEM((JB, wide), F32),
            pltpu.VMEM((JB, wide), F32),
            pltpu.VMEM((8, wide), F32),
        ],
        compiler_params=pltpu.CompilerParams(vmem_limit_bytes=10 << 20),
    )(first, near_lists, near_counts, cntw, posw, anw, densw)
    nxt, hess = pl.pallas_call(
        functools.partial(finish_kernel, roles, devs),
        name="finish",
        out_shape=(
            jax.ShapeDtypeStruct((local, panels), F32),
            jax.ShapeDtypeStruct((1, krylov_basis.shape[0] + 1), F32),
        ),
        in_specs=[smem, smem, smem] + [vmem] * 10,
        out_specs=(vmem, vmem),
        scratch_shapes=[
            pltpu.VMEM((total, 1, 128), F32),
            dma((total,)),
            dma((total,)),
        ],
        compiler_params=pltpu.CompilerParams(
            collective_id=1, has_side_effects=True, vmem_limit_bytes=14 << 20
        ),
    )(
        panel_counts,
        group_lists,
        group_kinds,
        leaf_lists,
        leaf_kinds,
        momw,
        gmall,
        near,
        densw,
        krylov_basis,
        moment_maps,
        up_operators,
        far_operators,
    )
    return nxt, jnp.reshape(hess, (krylov_basis.shape[0] + 1,))


def solution(mesh):
    roles, devs = mesh.shape["role"], mesh.shape["dev"]
    return jax.shard_map(
        functools.partial(shards, roles, devs),
        mesh=mesh,
        in_specs=(
            P(AXES, None, None),
            P(AXES, None, None),
            P(AXES, None),
            P(AXES),
            P(AXES, None),
            P(AXES),
            P(AXES, None),
            P(AXES, None),
            P(AXES, None),
            P(AXES, None),
            P(AXES, None, None),
            P(AXES, None, None),
            P(),
            P(),
            P(None, AXES, None),
        ),
        out_specs=(P(AXES, None), P()),
        check_vma=False,
    )
```

```python
import functools

import jax
import jax.numpy as jnp
from jax import lax
from jax.experimental import pallas as pl
from jax.experimental.pallas import tpu as pltpu
from jax.sharding import PartitionSpec as P

RADIUS = 3
SIDES = 2 * RADIUS + 1
SOFTEN = 0.01
EPSILON = 1e-06
JB = 256
MESH = pl.DeviceIdType.MESH
NT = (((1,), (1,)), ((), ()))
NN = (((1,), (0,)), ((), ()))
TN = (((0,), (0,)), ((), ()))
F32 = jnp.float32
BF16 = jnp.bfloat16
AXES = ("role", "dev")


def mm(a, b, dims):
    return lax.dot_general(a, b, dims, preferred_element_type=F32)


def row_is(shape, k):
    return lax.broadcasted_iota(jnp.int32, shape, 0) == k


def place(roles, devs):
    me = lax.axis_index("role") * devs + lax.axis_index("dev")
    return me, roles * devs


def coords(linear, devs):
    return (linear // devs, lax.rem(linear, devs))


def greet(me, total, devs):
    barrier = pltpu.get_barrier_semaphore()

    def body(i, carry):
        pl.semaphore_signal(
            barrier,
            inc=1,
            device_id=coords(lax.rem(me + i, total), devs),
            device_id_type=MESH,
        )
        return carry

    lax.fori_loop(1, total, body, 0)
    return barrier


def live_mask(cnt_ref, shape):
    rows = lax.broadcasted_iota(jnp.int32, shape, 0)
    limit = jnp.zeros(shape, jnp.int32)
    for c in range(shape[0]):
        limit = jnp.where(rows == c, cnt_ref[c], limit)
    return lax.broadcasted_iota(jnp.int32, shape, 1) < limit


def halves(x):
    hi = x.astype(BF16).astype(F32)
    return jnp.concatenate([hi, x - hi], axis=0).astype(BF16)


def source_kernel(
    roles,
    devs,
    cnt,
    pos,
    nrm,
    area,
    kry,
    binv,
    maps,
    ups,
    posw,
    anw,
    cntw,
    momw,
    gmall,
    nrm_v,
    area_v,
    kry_v,
    binv_v,
    maps_v,
    ups_v,
    local_sem,
    big_sem,
    send_sem,
    recv_sem,
    gsend,
    grecv,
):
    me, total = place(roles, devs)
    local, panels = area.shape
    coeffs = maps_v.shape[1]
    copies = []
    for c in range(local):
        copies.append(pltpu.make_async_copy(binv.at[c], binv_v.at[c], big_sem.at[c]))
    map_copy = pltpu.make_async_copy(maps, maps_v, local_sem.at[0])
    up_copy = pltpu.make_async_copy(ups, ups_v, local_sem.at[1])
    small = [
        pltpu.make_async_copy(pos, posw.at[RADIUS], local_sem.at[2]),
        pltpu.make_async_copy(nrm, nrm_v, local_sem.at[3]),
        pltpu.make_async_copy(area, area_v, local_sem.at[4]),
        pltpu.make_async_copy(kry.at[kry.shape[0] - 1], kry_v, local_sem.at[5]),
    ]
    for copy in small + copies:
        copy.start()
    map_copy.start()
    up_copy.start()
    barrier = greet(me, total, devs)
    for copy in small:
        copy.wait()
    parts = [nrm_v[a] * area_v[...] for a in range(3)]
    anw[RADIUS, : 3 * local] = jnp.concatenate(parts, axis=0).astype(BF16)
    lane = lax.broadcasted_iota(jnp.int32, (1, 128), 1)
    counts = jnp.zeros((1, 128), jnp.int32)
    for c in range(local):
        counts = jnp.where(lane == c, cnt[c], counts)
    cntw[RADIUS] = counts
    pl.semaphore_wait(barrier, total - 1)

    def to_neighbours(ref, kind, rows=None):
        made = []

        def slot(side):
            return ref.at[side] if rows is None else ref.at[side, rows]

        for n, d in enumerate([1, -1, 2, -2, 3, -3]):
            made.append(
                pltpu.make_async_remote_copy(
                    src_ref=slot(RADIUS),
                    dst_ref=slot(RADIUS - d),
                    send_sem=send_sem.at[kind, n],
                    recv_sem=recv_sem.at[kind, n],
                    device_id=coords(lax.rem(me + d + total, total), devs),
                    device_id_type=MESH,
                )
            )
        for copy in made:
            copy.start()
        return made

    sent = to_neighbours(posw, 0) + to_neighbours(anw, 4, pl.ds(0, 3 * local)) + to_neighbours(cntw, 1)
    live = live_mask(cnt, (local, panels))
    current = kry_v[...].astype(BF16)
    density = jnp.zeros((local, panels), F32)
    for c in range(local):
        copies[c].wait()
        found = mm(current, binv_v[c], NT)
        density = jnp.where(row_is(found.shape, c), found, density)
    rounded = jnp.where(live, density, 0.0).astype(BF16)
    anw[RADIUS, 3 * local :] = rounded
    sent += to_neighbours(anw, 2, pl.ds(3 * local, local))
    map_copy.wait()
    moments = jnp.zeros((local, coeffs), F32)
    for c in range(local):
        found = mm(rounded, maps_v[c], NT)
        moments = jnp.where(row_is(found.shape, c), found, moments)
    moments = moments.astype(BF16)
    momw[RADIUS] = moments
    sent += to_neighbours(momw, 3)
    up_copy.wait()
    merged = jnp.zeros((local, coeffs), F32)
    for k in range(local):
        found = mm(moments, ups_v[k], NT)
        merged = jnp.where(row_is(found.shape, k), found, merged)
    gmall[me] = jnp.sum(merged, axis=0, keepdims=True)

    def group_copy(i):
        return pltpu.make_async_remote_copy(
            src_ref=gmall.at[me],
            dst_ref=gmall.at[me],
            send_sem=gsend.at[i],
            recv_sem=grecv.at[i],
            device_id=coords(lax.rem(me + i, total), devs),
            device_id_type=MESH,
        )

    def start_one(i, carry):
        group_copy(i).start()
        return carry

    def wait_one(i, carry):
        source = lax.rem(me - i + total, total)
        pltpu.make_async_remote_copy(
            src_ref=gmall.at[me],
            dst_ref=gmall.at[source],
            send_sem=gsend.at[i],
            recv_sem=grecv.at[i],
            device_id=coords(lax.rem(me + i, total), devs),
            device_id_type=MESH,
        ).wait()
        return carry

    lax.fori_loop(1, total, start_one, 0)
    for copy in sent:
        copy.wait()
    lax.fori_loop(1, total, wait_one, 0)


def splits(x):
    hi = x.astype(BF16).astype(F32)
    rest = x - hi
    mid = rest.astype(BF16).astype(F32)
    return hi, mid, rest - mid


def near_kernel(
    first, near, used, cntw, posw, anw, out, src_sq, src_pr, weight, sq0, pr0, sq1, pr1, acc
):
    local, panels = out.shape
    chunks = panels // 128
    shape = (8, panels)
    rows = lax.broadcasted_iota(jnp.int32, shape, 0)
    for side in range(SIDES):
        products_an = anw[side].astype(F32)
        dens = products_an[3 * local :]
        for a in range(3):
            weight[side, a] = products_an[a * local : (a + 1) * local] * dens

    def vectors(ref, side, inner):
        return [
            jnp.broadcast_to(ref[side, a, pl.ds(inner, 1), :], shape) for a in range(3)
        ]

    def stack(values):
        feat = jnp.zeros(shape, F32)
        for k, value in enumerate(values):
            feat = jnp.where(rows == k, value, feat)
        return feat

    def pack(feat, order):
        parts = splits(feat)
        return jnp.concatenate([parts[k] for k in order], axis=0).astype(BF16)

    def cluster_body(c, carry):
        x0, x1, x2 = vectors(posw, RADIUS, c)
        norm = x0 * x0 + x1 * x1 + x2 * x2
        target = pack(stack([x0, x1, x2, 1.0, norm]), (0, 1, 0, 2, 0, 1))

        def slot_body(s, offset):
            listed = near[c, jnp.maximum(s - 1, 0)] - first[0]
            w = jnp.where(s == 0, RADIUS * local + c, listed)
            side = w // local
            inner = lax.rem(w, local)
            y0, y1, y2 = vectors(posw, side, inner)
            w0, w1, w2 = vectors(weight, side, inner)
            norm = y0 * y0 + y1 * y1 + y2 * y2 + SOFTEN
            inside = -(y0 * w0 + y1 * w1 + y2 * w2)
            order = (0, 0, 1, 0, 2, 1)
            sq = pack(stack([-2.0 * y0, -2.0 * y1, -2.0 * y2, norm, 1.0]), order)
            pr = pack(stack([w0, w1, w2, inside]), order)
            count = (cntw[side, 0, inner] + 127) // 128
            for b in range(chunks):
                src_sq[offset + b] = sq[:, b * 128 : (b + 1) * 128]
                src_pr[offset + b] = pr[:, b * 128 : (b + 1) * 128]
            return offset + count

        end = lax.fori_loop(0, used[c] + 1, slot_body, 0)
        pad_rows = lax.broadcasted_iota(jnp.int32, (48, 128), 0)
        for b in range(3):
            src_sq[end + b] = jnp.where(pad_rows == 3, 1.0, 0.0).astype(BF16)
            src_pr[end + b] = jnp.zeros((48, 128), BF16)

        def products(block, sq_ref, pr_ref):
            for half in range(2):
                part = pl.ds(half * 128, 128)
                sq_ref[part, :] = mm(src_sq[2 * block + half], target, TN)
                pr_ref[part, :] = mm(src_pr[2 * block + half], target, TN)

        def consume(sq_ref, pr_ref):
            for r in range(0, panels, 256):
                total = acc[:, r : r + 256]
                for j in range(0, JB, 8):
                    inverse = lax.rsqrt(sq_ref[j : j + 8, r : r + 256])
                    total = total + pr_ref[j : j + 8, r : r + 256] * inverse * (
                        inverse * inverse
                    )
                acc[:, r : r + 256] = total

        acc[...] = jnp.zeros(acc.shape, F32)
        blocks = (end + 1) // 2
        products(0, sq0, pr0)

        def pair_body(t, carry):
            products(2 * t + 1, sq1, pr1)
            consume(sq0, pr0)
            products(2 * t + 2, sq0, pr0)
            consume(sq1, pr1)
            return carry

        lax.fori_loop(0, blocks // 2, pair_body, 0)

        @pl.when(lax.rem(blocks, 2) == 1)
        def _():
            consume(sq0, pr0)

        out[pl.ds(c, 1), :] = jnp.sum(acc[...], axis=0, keepdims=True)
        return carry

    lax.fori_loop(0, local, cluster_body, 0)


def finish_kernel(
    roles,
    devs,
    cnt,
    glist,
    gkind,
    llist,
    lkind,
    momw,
    gmall,
    near,
    anw,
    kry,
    maps_v,
    ups_v,
    fars_v,
    nxt,
    hess,
    red,
    send_sem,
    recv_sem,
):
    me, total = place(roles, devs)
    local, panels = near.shape
    coeffs = maps_v.shape[1]
    kinds = fars_v.shape[1]
    window = SIDES * local
    barrier = greet(me, total, devs)

    groups = gmall[...].reshape(total, coeffs)
    g_rows = lax.broadcasted_iota(jnp.int32, (kinds, total), 0)
    g_lanes = lax.broadcasted_iota(jnp.int32, (kinds, total), 1)
    g_hot = jnp.zeros((kinds, total), F32)
    for n in range(glist.shape[1]):
        g_hot += jnp.where((g_rows == gkind[0, n]) & (g_lanes == glist[0, n]), 1.0, 0.0)
    g_hot = g_hot.astype(BF16)
    hi, mid, low = splits(groups)
    g_sum = mm(g_hot, hi.astype(BF16), NN) + mm(g_hot, mid.astype(BF16), NN)
    g_sum += mm(g_hot, low.astype(BF16), NN)
    g_both = halves(g_sum)

    lanes = lax.broadcasted_iota(jnp.int32, (local, window), 1)
    base = (me - RADIUS) * local
    hots = [jnp.zeros((local, window), F32) for _ in range(kinds)]
    for n in range(llist.shape[1]):
        hit = lanes == (llist[:, n : n + 1] - base)
        kind = jnp.broadcast_to(lkind[:, n : n + 1], (local, window))
        for o in range(kinds):
            hots[o] = hots[o] + jnp.where(hit & (kind == o), 1.0, 0.0)
    hot = jnp.concatenate(hots, axis=0).astype(BF16)
    held = jnp.concatenate([momw[side].astype(F32) for side in range(SIDES)], axis=0)
    summed = mm(hot, held.astype(BF16), NN)

    g_parts = jnp.zeros((kinds, coeffs), F32)
    for o in range(kinds):
        found = mm(g_both, fars_v[1, o], NT)
        found = found[:kinds] + found[kinds:]
        g_parts = jnp.where(row_is(found.shape, o), found, g_parts)
    g_local = jnp.sum(g_parts, axis=0, keepdims=True).astype(BF16)
    leaf = jnp.zeros((local, coeffs), F32)
    for o in range(kinds):
        found = mm(halves(summed[o * local : (o + 1) * local]), fars_v[0, o], NT)
        leaf = leaf + found[:local] + found[local:]
    g_wide = jnp.broadcast_to(g_local.astype(F32), (local, coeffs)).astype(BF16)
    down = jnp.zeros((local, coeffs), F32)
    for k in range(local):
        found = mm(g_wide, ups_v[k], NN)
        down = jnp.where(row_is(found.shape, k), found, down)
    leaf = (leaf + down).astype(BF16)
    far = jnp.zeros((local, panels), F32)
    for c in range(local):
        found = mm(leaf, maps_v[c], NN)
        far = jnp.where(row_is(found.shape, c), found, far)
    live = live_mask(cnt, (local, panels))
    image = jnp.where(live, 0.5 * anw[RADIUS].astype(F32)[3 * local :] + near[...] + far, 0.0)

    lane = lax.broadcasted_iota(jnp.int32, (1, 128), 1)
    count = kry.shape[0]
    row = jnp.zeros((1, 128), F32)
    for k in range(count + 1):
        part = image * (kry[k] if k < count else image)
        value = jnp.sum(jnp.sum(part, axis=0, keepdims=True), axis=1, keepdims=True)
        row = jnp.where(lane == k, value, row)
    red[me] = row
    pl.semaphore_wait(barrier, total - 1)

    def one(i):
        source = lax.rem(me - i + total, total)
        target = coords(lax.rem(me + i, total), devs)

        def copy(dst):
            return pltpu.make_async_remote_copy(
                src_ref=red.at[me],
                dst_ref=red.at[dst],
                send_sem=send_sem.at[i],
                recv_sem=recv_sem.at[i],
                device_id=target,
                device_id_type=MESH,
            )

        return copy, source

    def start_one(i, carry):
        one(i)[0](me).start()
        return carry

    def wait_one(i, carry):
        copy, source = one(i)
        copy(source).wait()
        return carry

    lax.fori_loop(1, total, start_one, 0)
    lax.fori_loop(1, total, wait_one, 0)
    scale = 1.0 / (total * local * panels)
    sums = jnp.sum(red[...], axis=0) * scale
    rest = image
    energy = sums[:, count : count + 1]
    for k in range(count):
        c_k = sums[:, k : k + 1]
        rest = rest - c_k * kry[k]
        energy = energy - c_k * c_k
    height = jnp.sqrt(energy + EPSILON)
    nxt[...] = rest / height
    hess[...] = jnp.where(lane == count, height, sums)[:, : count + 1]


def shards(
    roles,
    devs,
    positions,
    normals,
    panel_areas,
    panel_counts,
    near_lists,
    near_counts,
    leaf_lists,
    leaf_kinds,
    group_lists,
    group_kinds,
    block_inverse,
    moment_maps,
    up_operators,
    far_operators,
    krylov_basis,
):
    local, _, panels = positions.shape
    coeffs = moment_maps.shape[1]
    total = roles * devs
    vmem = pl.BlockSpec(memory_space=pltpu.VMEM)
    smem = pl.BlockSpec(memory_space=pltpu.SMEM)
    hbm = pl.BlockSpec(memory_space=pltpu.HBM)
    dma = pltpu.SemaphoreType.DMA
    posw, anw, cntw, momw, gmall = pl.pallas_call(
        functools.partial(source_kernel, roles, devs),
        name="sources",
        out_shape=(
            jax.ShapeDtypeStruct((SIDES, 3, local, panels), F32),
            jax.ShapeDtypeStruct((SIDES, 4 * local, panels), BF16),
            jax.ShapeDtypeStruct((SIDES, 1, 128), jnp.int32),
            jax.ShapeDtypeStruct((SIDES, local, coeffs), BF16),
            jax.ShapeDtypeStruct((total, 1, coeffs), F32),
        ),
        in_specs=[smem] + [hbm] * 7,
        out_specs=(vmem,) * 5,
        scratch_shapes=[
            pltpu.VMEM((3, local, panels), F32),
            pltpu.VMEM((local, panels), F32),
            pltpu.VMEM((local, panels), F32),
            pltpu.VMEM(block_inverse.shape, BF16),
            pltpu.VMEM(moment_maps.shape, BF16),
            pltpu.VMEM(up_operators.shape, BF16),
            dma((6,)),
            dma((local,)),
            dma((5, 6)),
            dma((5, 6)),
            dma((total,)),
            dma((total,)),
        ],
        compiler_params=pltpu.CompilerParams(
            collective_id=0, has_side_effects=True, vmem_limit_bytes=62 << 20
        ),
    )(
        panel_counts,
        jnp.transpose(positions, (1, 0, 2)),
        jnp.transpose(normals, (1, 0, 2)),
        panel_areas,
        krylov_basis,
        block_inverse,
        moment_maps,
        up_operators,
    )
    own = lax.axis_index(AXES)
    first = jnp.reshape((own - RADIUS) * local, (1,)).astype(jnp.int32)
    room = (near_lists.shape[1] + 1) * (panels // 128) + 8
    near = pl.pallas_call(
        near_kernel,
        name="near",
        cost_estimate=pl.CostEstimate(
            flops=40 * local * panels * panels * (near_lists.shape[1] + 1),
            bytes_accessed=48 * local * panels * SIDES,
            transcendentals=local * panels * panels * (near_lists.shape[1] + 1),
        ),
        out_shape=jax.ShapeDtypeStruct((local, panels), F32),
        in_specs=[smem, smem, smem, smem, vmem, vmem],
        out_specs=vmem,
        scratch_shapes=[
            pltpu.VMEM((room, 48, 128), BF16),
            pltpu.VMEM((room, 48, 128), BF16),
            pltpu.VMEM((SIDES, 3, local, panels), F32),
            pltpu.VMEM((JB, panels), F32),
            pltpu.VMEM((JB, panels), F32),
            pltpu.VMEM((JB, panels), F32),
            pltpu.VMEM((JB, panels), F32),
            pltpu.VMEM((8, panels), F32),
        ],
        compiler_params=pltpu.CompilerParams(vmem_limit_bytes=10 << 20),
    )(first, near_lists, near_counts, cntw, posw, anw)
    nxt, hess = pl.pallas_call(
        functools.partial(finish_kernel, roles, devs),
        name="finish",
        out_shape=(
            jax.ShapeDtypeStruct((local, panels), F32),
            jax.ShapeDtypeStruct((1, krylov_basis.shape[0] + 1), F32),
        ),
        in_specs=[smem, smem, smem] + [vmem] * 10,
        out_specs=(vmem, vmem),
        scratch_shapes=[
            pltpu.VMEM((total, 1, 128), F32),
            dma((total,)),
            dma((total,)),
        ],
        compiler_params=pltpu.CompilerParams(
            collective_id=1, has_side_effects=True, vmem_limit_bytes=14 << 20
        ),
    )(
        panel_counts,
        group_lists,
        group_kinds,
        leaf_lists,
        leaf_kinds,
        momw,
        gmall,
        near,
        anw,
        krylov_basis,
        moment_maps,
        up_operators,
        far_operators,
    )
    return nxt, jnp.reshape(hess, (krylov_basis.shape[0] + 1,))


def solution(mesh):
    roles, devs = mesh.shape["role"], mesh.shape["dev"]
    return jax.shard_map(
        functools.partial(shards, roles, devs),
        mesh=mesh,
        in_specs=(
            P(AXES, None, None),
            P(AXES, None, None),
            P(AXES, None),
            P(AXES),
            P(AXES, None),
            P(AXES),
            P(AXES, None),
            P(AXES, None),
            P(AXES, None),
            P(AXES, None),
            P(AXES, None, None),
            P(AXES, None, None),
            P(),
            P(),
            P(None, AXES, None),
        ),
        out_specs=(P(AXES, None), P()),
        check_vma=False,
    )
```

```python
import functools

import jax
import jax.numpy as jnp
from jax import lax
from jax.experimental import pallas as pl
from jax.experimental.pallas import tpu as pltpu
from jax.sharding import PartitionSpec as P

RADIUS = 3
SIDES = 2 * RADIUS + 1
SOFTEN = 0.01
EPSILON = 1e-06
JB = 256
MESH = pl.DeviceIdType.MESH
NT = (((1,), (1,)), ((), ()))
NN = (((1,), (0,)), ((), ()))
TN = (((0,), (0,)), ((), ()))
F32 = jnp.float32
BF16 = jnp.bfloat16
AXES = ("role", "dev")


def mm(a, b, dims):
    return lax.dot_general(a, b, dims, preferred_element_type=F32)


def row_is(shape, k):
    return lax.broadcasted_iota(jnp.int32, shape, 0) == k


def place(roles, devs):
    me = lax.axis_index("role") * devs + lax.axis_index("dev")
    return me, roles * devs


def coords(linear, devs):
    return (linear // devs, lax.rem(linear, devs))


def greet(me, total, devs):
    barrier = pltpu.get_barrier_semaphore()

    def body(i, carry):
        pl.semaphore_signal(
            barrier,
            inc=1,
            device_id=coords(lax.rem(me + i, total), devs),
            device_id_type=MESH,
        )
        return carry

    lax.fori_loop(1, total, body, 0)
    return barrier


def live_mask(cnt_ref, shape):
    rows = lax.broadcasted_iota(jnp.int32, shape, 0)
    limit = jnp.zeros(shape, jnp.int32)
    for c in range(shape[0]):
        limit = jnp.where(rows == c, cnt_ref[c], limit)
    return lax.broadcasted_iota(jnp.int32, shape, 1) < limit


def halves(x):
    hi = x.astype(BF16).astype(F32)
    return jnp.concatenate([hi, x - hi], axis=0).astype(BF16)


def source_kernel(
    roles,
    devs,
    cnt,
    pos,
    nrm,
    area,
    kry,
    binv,
    maps,
    ups,
    posw,
    anw,
    cntw,
    momw,
    gmall,
    nrm_v,
    area_v,
    kry_v,
    binv_v,
    maps_v,
    ups_v,
    local_sem,
    big_sem,
    send_sem,
    recv_sem,
    gsend,
    grecv,
):
    me, total = place(roles, devs)
    local, panels = area.shape
    coeffs = maps_v.shape[1]
    copies = []
    for c in range(local):
        copies.append(pltpu.make_async_copy(binv.at[c], binv_v.at[c], big_sem.at[c]))
    map_copy = pltpu.make_async_copy(maps, maps_v, local_sem.at[0])
    up_copy = pltpu.make_async_copy(ups, ups_v, local_sem.at[1])
    small = [
        pltpu.make_async_copy(pos, posw.at[RADIUS], local_sem.at[2]),
        pltpu.make_async_copy(nrm, nrm_v, local_sem.at[3]),
        pltpu.make_async_copy(area, area_v, local_sem.at[4]),
        pltpu.make_async_copy(kry.at[kry.shape[0] - 1], kry_v, local_sem.at[5]),
    ]
    for copy in small + copies:
        copy.start()
    map_copy.start()
    up_copy.start()
    barrier = greet(me, total, devs)
    for copy in small:
        copy.wait()
    parts = [nrm_v[a] * area_v[...] for a in range(3)]
    anw[RADIUS, : 3 * local] = jnp.concatenate(parts, axis=0).astype(BF16)
    lane = lax.broadcasted_iota(jnp.int32, (1, 128), 1)
    counts = jnp.zeros((1, 128), jnp.int32)
    for c in range(local):
        counts = jnp.where(lane == c, cnt[c], counts)
    cntw[RADIUS] = counts
    current = kry_v[...].astype(BF16)
    density = jnp.zeros((local, panels), F32)
    for c in range(local // 2):
        copies[c].wait()
        found = mm(current, binv_v[c], NT)
        density = jnp.where(row_is(found.shape, c), found, density)
    pl.semaphore_wait(barrier, total - 1)

    def to_neighbours(ref, kind, rows=None):
        made = []

        def slot(side):
            return ref.at[side] if rows is None else ref.at[side, rows]

        for n, d in enumerate([1, -1, 2, -2, 3, -3]):
            made.append(
                pltpu.make_async_remote_copy(
                    src_ref=slot(RADIUS),
                    dst_ref=slot(RADIUS - d),
                    send_sem=send_sem.at[kind, n],
                    recv_sem=recv_sem.at[kind, n],
                    device_id=coords(lax.rem(me + d + total, total), devs),
                    device_id_type=MESH,
                )
            )
        for copy in made:
            copy.start()
        return made

    sent = to_neighbours(posw, 0) + to_neighbours(anw, 4, pl.ds(0, 3 * local)) + to_neighbours(cntw, 1)
    live = live_mask(cnt, (local, panels))
    for c in range(local // 2, local):
        copies[c].wait()
        found = mm(current, binv_v[c], NT)
        density = jnp.where(row_is(found.shape, c), found, density)
    rounded = jnp.where(live, density, 0.0).astype(BF16)
    anw[RADIUS, 3 * local :] = rounded
    sent += to_neighbours(anw, 2, pl.ds(3 * local, local))
    map_copy.wait()
    moments = jnp.zeros((local, coeffs), F32)
    for c in range(local):
        found = mm(rounded, maps_v[c], NT)
        moments = jnp.where(row_is(found.shape, c), found, moments)
    moments = moments.astype(BF16)
    momw[RADIUS] = moments
    sent += to_neighbours(momw, 3)
    up_copy.wait()
    merged = jnp.zeros((local, coeffs), F32)
    for k in range(local):
        found = mm(moments, ups_v[k], NT)
        merged = jnp.where(row_is(found.shape, k), found, merged)
    gmall[me] = jnp.sum(merged, axis=0, keepdims=True)

    def group_copy(i):
        return pltpu.make_async_remote_copy(
            src_ref=gmall.at[me],
            dst_ref=gmall.at[me],
            send_sem=gsend.at[i],
            recv_sem=grecv.at[i],
            device_id=coords(lax.rem(me + i, total), devs),
            device_id_type=MESH,
        )

    def start_one(i, carry):
        group_copy(i).start()
        return carry

    def wait_one(i, carry):
        source = lax.rem(me - i + total, total)
        pltpu.make_async_remote_copy(
            src_ref=gmall.at[me],
            dst_ref=gmall.at[source],
            send_sem=gsend.at[i],
            recv_sem=grecv.at[i],
            device_id=coords(lax.rem(me + i, total), devs),
            device_id_type=MESH,
        ).wait()
        return carry

    lax.fori_loop(1, total, start_one, 0)
    for copy in sent:
        copy.wait()
    lax.fori_loop(1, total, wait_one, 0)


def splits(x):
    hi = x.astype(BF16).astype(F32)
    rest = x - hi
    mid = rest.astype(BF16).astype(F32)
    return hi, mid, rest - mid


def near_kernel(
    first, near, used, cntw, posw, anw, out, src_sq, src_pr, weight, sq0, pr0, sq1, pr1, acc
):
    local, panels = out.shape
    chunks = panels // 128
    shape = (8, panels)
    rows = lax.broadcasted_iota(jnp.int32, shape, 0)
    for side in range(SIDES):
        products_an = anw[side].astype(F32)
        dens = products_an[3 * local :]
        for a in range(3):
            weight[side, a] = products_an[a * local : (a + 1) * local] * dens

    def vectors(ref, side, inner):
        return [
            jnp.broadcast_to(ref[side, a, pl.ds(inner, 1), :], shape) for a in range(3)
        ]

    def stack(values):
        feat = jnp.zeros(shape, F32)
        for k, value in enumerate(values):
            feat = jnp.where(rows == k, value, feat)
        return feat

    def pack(feat, order):
        parts = splits(feat)
        return jnp.concatenate([parts[k] for k in order], axis=0).astype(BF16)

    def cluster_body(c, carry):
        x0, x1, x2 = vectors(posw, RADIUS, c)
        norm = x0 * x0 + x1 * x1 + x2 * x2
        target = pack(stack([x0, x1, x2, 1.0, norm]), (0, 1, 0, 2, 0, 1))

        def slot_body(s, offset):
            listed = near[c, jnp.maximum(s - 1, 0)] - first[0]
            w = jnp.where(s == 0, RADIUS * local + c, listed)
            side = w // local
            inner = lax.rem(w, local)
            y0, y1, y2 = vectors(posw, side, inner)
            w0, w1, w2 = vectors(weight, side, inner)
            norm = y0 * y0 + y1 * y1 + y2 * y2 + SOFTEN
            inside = -(y0 * w0 + y1 * w1 + y2 * w2)
            order = (0, 0, 1, 0, 2, 1)
            sq = pack(stack([-2.0 * y0, -2.0 * y1, -2.0 * y2, norm, 1.0]), order)
            pr = pack(stack([w0, w1, w2, inside]), order)
            count = (cntw[side, 0, inner] + 127) // 128
            for b in range(chunks):
                src_sq[offset + b] = sq[:, b * 128 : (b + 1) * 128]
                src_pr[offset + b] = pr[:, b * 128 : (b + 1) * 128]
            return offset + count

        end = lax.fori_loop(0, used[c] + 1, slot_body, 0)
        pad_rows = lax.broadcasted_iota(jnp.int32, (48, 128), 0)
        for b in range(3):
            src_sq[end + b] = jnp.where(pad_rows == 3, 1.0, 0.0).astype(BF16)
            src_pr[end + b] = jnp.zeros((48, 128), BF16)

        def products(block, sq_ref, pr_ref):
            for half in range(2):
                part = pl.ds(half * 128, 128)
                sq_ref[part, :] = mm(src_sq[2 * block + half], target, TN)
                pr_ref[part, :] = mm(src_pr[2 * block + half], target, TN)

        def consume(sq_ref, pr_ref):
            for r in range(0, panels, 256):
                total = acc[:, r : r + 256]
                for j in range(0, JB, 8):
                    inverse = lax.rsqrt(sq_ref[j : j + 8, r : r + 256])
                    total = total + pr_ref[j : j + 8, r : r + 256] * inverse * (
                        inverse * inverse
                    )
                acc[:, r : r + 256] = total

        acc[...] = jnp.zeros(acc.shape, F32)
        blocks = (end + 1) // 2
        products(0, sq0, pr0)

        def pair_body(t, carry):
            products(2 * t + 1, sq1, pr1)
            consume(sq0, pr0)
            products(2 * t + 2, sq0, pr0)
            consume(sq1, pr1)
            return carry

        lax.fori_loop(0, blocks // 2, pair_body, 0)

        @pl.when(lax.rem(blocks, 2) == 1)
        def _():
            consume(sq0, pr0)

        out[pl.ds(c, 1), :] = jnp.sum(acc[...], axis=0, keepdims=True)
        return carry

    lax.fori_loop(0, local, cluster_body, 0)


def finish_kernel(
    roles,
    devs,
    cnt,
    glist,
    gkind,
    llist,
    lkind,
    momw,
    gmall,
    near,
    anw,
    kry,
    maps_v,
    ups_v,
    fars_v,
    nxt,
    hess,
    red,
    send_sem,
    recv_sem,
):
    me, total = place(roles, devs)
    local, panels = near.shape
    coeffs = maps_v.shape[1]
    kinds = fars_v.shape[1]
    window = SIDES * local
    barrier = greet(me, total, devs)

    groups = gmall[...].reshape(total, coeffs)
    g_rows = lax.broadcasted_iota(jnp.int32, (kinds, total), 0)
    g_lanes = lax.broadcasted_iota(jnp.int32, (kinds, total), 1)
    g_hot = jnp.zeros((kinds, total), F32)
    for n in range(glist.shape[1]):
        g_hot += jnp.where((g_rows == gkind[0, n]) & (g_lanes == glist[0, n]), 1.0, 0.0)
    g_hot = g_hot.astype(BF16)
    hi, mid, low = splits(groups)
    g_sum = mm(g_hot, hi.astype(BF16), NN) + mm(g_hot, mid.astype(BF16), NN)
    g_sum += mm(g_hot, low.astype(BF16), NN)
    g_both = halves(g_sum)

    lanes = lax.broadcasted_iota(jnp.int32, (local, window), 1)
    base = (me - RADIUS) * local
    hots = [jnp.zeros((local, window), F32) for _ in range(kinds)]
    for n in range(llist.shape[1]):
        hit = lanes == (llist[:, n : n + 1] - base)
        kind = jnp.broadcast_to(lkind[:, n : n + 1], (local, window))
        for o in range(kinds):
            hots[o] = hots[o] + jnp.where(hit & (kind == o), 1.0, 0.0)
    hot = jnp.concatenate(hots, axis=0).astype(BF16)
    held = jnp.concatenate([momw[side].astype(F32) for side in range(SIDES)], axis=0)
    summed = mm(hot, held.astype(BF16), NN)

    g_parts = jnp.zeros((kinds, coeffs), F32)
    for o in range(kinds):
        found = mm(g_both, fars_v[1, o], NT)
        found = found[:kinds] + found[kinds:]
        g_parts = jnp.where(row_is(found.shape, o), found, g_parts)
    g_local = jnp.sum(g_parts, axis=0, keepdims=True).astype(BF16)
    leaf = jnp.zeros((local, coeffs), F32)
    for o in range(kinds):
        found = mm(halves(summed[o * local : (o + 1) * local]), fars_v[0, o], NT)
        leaf = leaf + found[:local] + found[local:]
    g_wide = jnp.broadcast_to(g_local.astype(F32), (local, coeffs)).astype(BF16)
    down = jnp.zeros((local, coeffs), F32)
    for k in range(local):
        found = mm(g_wide, ups_v[k], NN)
        down = jnp.where(row_is(found.shape, k), found, down)
    leaf = (leaf + down).astype(BF16)
    far = jnp.zeros((local, panels), F32)
    for c in range(local):
        found = mm(leaf, maps_v[c], NN)
        far = jnp.where(row_is(found.shape, c), found, far)
    live = live_mask(cnt, (local, panels))
    image = jnp.where(live, 0.5 * anw[RADIUS].astype(F32)[3 * local :] + near[...] + far, 0.0)

    lane = lax.broadcasted_iota(jnp.int32, (1, 128), 1)
    count = kry.shape[0]
    row = jnp.zeros((1, 128), F32)
    for k in range(count + 1):
        part = image * (kry[k] if k < count else image)
        value = jnp.sum(jnp.sum(part, axis=0, keepdims=True), axis=1, keepdims=True)
        row = jnp.where(lane == k, value, row)
    red[me] = row
    pl.semaphore_wait(barrier, total - 1)

    def one(i):
        source = lax.rem(me - i + total, total)
        target = coords(lax.rem(me + i, total), devs)

        def copy(dst):
            return pltpu.make_async_remote_copy(
                src_ref=red.at[me],
                dst_ref=red.at[dst],
                send_sem=send_sem.at[i],
                recv_sem=recv_sem.at[i],
                device_id=target,
                device_id_type=MESH,
            )

        return copy, source

    def start_one(i, carry):
        one(i)[0](me).start()
        return carry

    def wait_one(i, carry):
        copy, source = one(i)
        copy(source).wait()
        return carry

    lax.fori_loop(1, total, start_one, 0)
    lax.fori_loop(1, total, wait_one, 0)
    scale = 1.0 / (total * local * panels)
    sums = jnp.sum(red[...], axis=0) * scale
    rest = image
    energy = sums[:, count : count + 1]
    for k in range(count):
        c_k = sums[:, k : k + 1]
        rest = rest - c_k * kry[k]
        energy = energy - c_k * c_k
    height = jnp.sqrt(energy + EPSILON)
    nxt[...] = rest / height
    hess[...] = jnp.where(lane == count, height, sums)[:, : count + 1]


def shards(
    roles,
    devs,
    positions,
    normals,
    panel_areas,
    panel_counts,
    near_lists,
    near_counts,
    leaf_lists,
    leaf_kinds,
    group_lists,
    group_kinds,
    block_inverse,
    moment_maps,
    up_operators,
    far_operators,
    krylov_basis,
):
    local, _, panels = positions.shape
    coeffs = moment_maps.shape[1]
    total = roles * devs
    vmem = pl.BlockSpec(memory_space=pltpu.VMEM)
    smem = pl.BlockSpec(memory_space=pltpu.SMEM)
    hbm = pl.BlockSpec(memory_space=pltpu.HBM)
    dma = pltpu.SemaphoreType.DMA
    posw, anw, cntw, momw, gmall = pl.pallas_call(
        functools.partial(source_kernel, roles, devs),
        name="sources",
        out_shape=(
            jax.ShapeDtypeStruct((SIDES, 3, local, panels), F32),
            jax.ShapeDtypeStruct((SIDES, 4 * local, panels), BF16),
            jax.ShapeDtypeStruct((SIDES, 1, 128), jnp.int32),
            jax.ShapeDtypeStruct((SIDES, local, coeffs), BF16),
            jax.ShapeDtypeStruct((total, 1, coeffs), F32),
        ),
        in_specs=[smem] + [hbm] * 7,
        out_specs=(vmem,) * 5,
        scratch_shapes=[
            pltpu.VMEM((3, local, panels), F32),
            pltpu.VMEM((local, panels), F32),
            pltpu.VMEM((local, panels), F32),
            pltpu.VMEM(block_inverse.shape, BF16),
            pltpu.VMEM(moment_maps.shape, BF16),
            pltpu.VMEM(up_operators.shape, BF16),
            dma((6,)),
            dma((local,)),
            dma((5, 6)),
            dma((5, 6)),
            dma((total,)),
            dma((total,)),
        ],
        compiler_params=pltpu.CompilerParams(
            collective_id=0, has_side_effects=True, vmem_limit_bytes=62 << 20
        ),
    )(
        panel_counts,
        jnp.transpose(positions, (1, 0, 2)),
        jnp.transpose(normals, (1, 0, 2)),
        panel_areas,
        krylov_basis,
        block_inverse,
        moment_maps,
        up_operators,
    )
    own = lax.axis_index(AXES)
    first = jnp.reshape((own - RADIUS) * local, (1,)).astype(jnp.int32)
    room = (near_lists.shape[1] + 1) * (panels // 128) + 8
    near = pl.pallas_call(
        near_kernel,
        name="near",
        cost_estimate=pl.CostEstimate(
            flops=40 * local * panels * panels * (near_lists.shape[1] + 1),
            bytes_accessed=48 * local * panels * SIDES,
            transcendentals=local * panels * panels * (near_lists.shape[1] + 1),
        ),
        out_shape=jax.ShapeDtypeStruct((local, panels), F32),
        in_specs=[smem, smem, smem, smem, vmem, vmem],
        out_specs=vmem,
        scratch_shapes=[
            pltpu.VMEM((room, 48, 128), BF16),
            pltpu.VMEM((room, 48, 128), BF16),
            pltpu.VMEM((SIDES, 3, local, panels), F32),
            pltpu.VMEM((JB, panels), F32),
            pltpu.VMEM((JB, panels), F32),
            pltpu.VMEM((JB, panels), F32),
            pltpu.VMEM((JB, panels), F32),
            pltpu.VMEM((8, panels), F32),
        ],
        compiler_params=pltpu.CompilerParams(vmem_limit_bytes=10 << 20),
    )(first, near_lists, near_counts, cntw, posw, anw)
    nxt, hess = pl.pallas_call(
        functools.partial(finish_kernel, roles, devs),
        name="finish",
        out_shape=(
            jax.ShapeDtypeStruct((local, panels), F32),
            jax.ShapeDtypeStruct((1, krylov_basis.shape[0] + 1), F32),
        ),
        in_specs=[smem, smem, smem] + [vmem] * 10,
        out_specs=(vmem, vmem),
        scratch_shapes=[
            pltpu.VMEM((total, 1, 128), F32),
            dma((total,)),
            dma((total,)),
        ],
        compiler_params=pltpu.CompilerParams(
            collective_id=1, has_side_effects=True, vmem_limit_bytes=14 << 20
        ),
    )(
        panel_counts,
        group_lists,
        group_kinds,
        leaf_lists,
        leaf_kinds,
        momw,
        gmall,
        near,
        anw,
        krylov_basis,
        moment_maps,
        up_operators,
        far_operators,
    )
    return nxt, jnp.reshape(hess, (krylov_basis.shape[0] + 1,))


def solution(mesh):
    roles, devs = mesh.shape["role"], mesh.shape["dev"]
    return jax.shard_map(
        functools.partial(shards, roles, devs),
        mesh=mesh,
        in_specs=(
            P(AXES, None, None),
            P(AXES, None, None),
            P(AXES, None),
            P(AXES),
            P(AXES, None),
            P(AXES),
            P(AXES, None),
            P(AXES, None),
            P(AXES, None),
            P(AXES, None),
            P(AXES, None, None),
            P(AXES, None, None),
            P(),
            P(),
            P(None, AXES, None),
        ),
        out_specs=(P(AXES, None), P()),
        check_vma=False,
    )
```
